256 devices in a mesh: req: 32 (over x, y, core), head: 8 (over z).
Axes of the slice: x: 4, y: 4, z: 8, core: 2. Of those that a mesh axis runs over, the one named last changes fastest.
Arguments:
- hidden_in: bfloat16 [8192, 4096], P('req', 'head'), may hold values from -6 to 6
- norm_gain: float32 [4096], replicated, may hold values from 0.25 to 1.75
- norm_shift: float32 [4096], replicated, may hold values from -3 to 3
- attend_weight: bfloat16 [4096, 3, 2048], P(None, None, 'head'), may hold values from -0.09375 to 0.09375
- output_weight: bfloat16 [2048, 4096], P('head'), may hold values from -0.125 to 0.125
- up_weight: bfloat16 [4096, 8192], P('req', 'head'), may hold values from -0.09375 to 0.09375
- up_bias: float32 [8192], P('head'), may hold values from -3 to 3
- down_weight: bfloat16 [8192, 4096], P('head', 'req'), may hold values from -0.0625 to 0.0625
- down_bias: float32 [4096], P('head'), may hold values from -3 to 3
- key_cache: bfloat16 [64, 1536, 2048], P('req', None, 'head'), may hold values from -160 to 160
- value_cache: bfloat16 [64, 1536, 2048], P('req', None, 'head'), may hold values from -5 to 5
- cached_len: int32 [64], P('req'), may hold values from 1 to 1536, as said below
Outputs:
- hidden_out: bfloat16 [8192, 4096], P('req', 'head')
- new_keys: bfloat16 [64, 128, 2048], P('req', None, 'head')
- new_values: bfloat16 [64, 128, 2048], P('req', None, 'head')
The draws below stay inside these ranges and needn't reach their ends.
Inputs may be any that keep to these rules, and one draw needn't show every extreme that they name: `cached_len`: each cached length is under 64 or between 768 and 1536; some request has exactly 1536.
All inputs are finite; a program needn't handle non-finite values.
Results may differ from the reference program's by a relative error of at most 0.012.
Values may be sent and summed in bfloat16 or wider, within the bound.
A program may use at most 128 MiB of HBM per device.

```python
import jax
import jax.numpy as jnp
from jax import lax

D = 4096
HD = 256
HEADS = 8
ROT = 64
FF = 8192
GROUP = 128
CMAX = 1536
SHORT = 64
REQS = 64
TOKENS = 8192


def draw_key_cache(key, part):
    first_key = jax.random.fold_in(jax.random.fold_in(key, 11), 0)
    base = jnp.clip(jax.random.normal(first_key, (REQS, CMAX, HEADS * HD), jnp.float32), -4.0, 4.0)
    return base.astype(jnp.bfloat16)


def draw_cached_len(key, part):
    coin_key, short_key, long_key, pick_key = jax.random.split(jax.random.fold_in(key, 23), 4)
    coins = jax.random.randint(coin_key, (REQS,), 0, 2)
    short_len = jax.random.randint(short_key, (REQS,), 1, SHORT)
    long_len = jax.random.randint(long_key, (REQS,), CMAX // 2, CMAX + 1)
    lengths = jnp.where(coins == 1, long_len, short_len)
    chosen = jax.random.randint(pick_key, (), 0, REQS)
    lengths = jnp.where(jnp.arange(REQS) == chosen, CMAX, lengths)
    return lengths.astype(jnp.int32)


def level_of(key, extent, cuts, low, top_value):
    factor_of, own = 1.0, jax.random.fold_in(key, 6)
    for dim, parts in cuts:
        draws = jnp.exp(jax.random.uniform(jax.random.fold_in(own, dim), (parts,), jnp.float32, low / len(cuts), top_value / len(cuts)))
        factor_of = factor_of * jnp.repeat(draws, extent[dim] // parts).reshape([-1 if axis == dim else 1 for axis in range(len(extent))])
    return factor_of


def gaussian(key, dims, deviation, most, cuts=(), held_as=jnp.bfloat16):
    loudness = level_of(key, dims, cuts, -0.22, 0.18) if cuts else 1.0
    drawn = jax.random.normal(key, dims, jnp.float32) * deviation * loudness
    return jnp.minimum(jnp.maximum(drawn, -most), most).astype(held_as)


def setup_inputs(seed: int = 0) -> dict:
    keys = jax.random.split(jax.random.key(seed), 13)
    return {
        "hidden_in": gaussian(keys[0], (TOKENS, D), 1.0, 6.0, ((0, 32), (1, 8))),
        "norm_gain": jnp.clip(1.0 + 0.15 * jax.random.normal(keys[1], (D,), jnp.float32), 0.25, 1.75),
        "norm_shift": gaussian(keys[2], (D,), 0.5, 3.0, (), jnp.float32),
        "attend_weight": gaussian(keys[3], (D, 3, HEADS * HD), D ** -0.5, 0.09375, ((2, 8),)),
        "output_weight": gaussian(keys[4], (HEADS * HD, D), (HEADS * HD) ** -0.5, 0.125, ((0, 8),)),
        "up_weight": gaussian(keys[5], (D, FF), D ** -0.5, 0.09375, ((0, 32), (1, 8))),
        "up_bias": gaussian(keys[6], (FF,), 0.5, 3.0, ((0, 8),), jnp.float32),
        "down_weight": gaussian(keys[7], (FF, D), FF ** -0.5, 0.0625, ((0, 8), (1, 32))),
        "down_bias": gaussian(keys[8], (D,), 0.5, 3.0, ((0, 8),), jnp.float32),
        "key_cache": draw_key_cache(jax.random.fold_in(keys[12], 71), 0),
        "value_cache": gaussian(keys[10], (REQS, CMAX, HEADS * HD), 1.0, 5.0, ((0, 32), (2, 8))),
        "cached_len": draw_cached_len(jax.random.fold_in(keys[12], 71), 0),
    }


epsilon = 1e-05

def layer_norm(values, gain_vec, shift_vec):
    floats = values.astype(jnp.float32)
    center = floats - lax.optimization_barrier(jnp.mean(floats, axis=-1, keepdims=True))
    spread = lax.optimization_barrier(jnp.mean(center * center, axis=-1, keepdims=True))
    return center * lax.rsqrt(spread + epsilon) * gain_vec + shift_vec

def rotate_pairs(tensor, positions):
    halves = ROT // 2
    frequency = 10000.0 ** (-(jnp.arange(halves, dtype=jnp.float32) * 2.0) / ROT)
    angles = positions.astype(jnp.float32)[:, :, None] * frequency
    cosine = jnp.cos(angles)[:, :, None, :]
    sine_part = jnp.sin(angles)[:, :, None, :]
    rotary = tensor[..., :ROT]
    even_part = rotary[..., 0::2]
    odd_part = rotary[..., 1::2]
    rotated = jnp.stack([even_part * cosine - odd_part * sine_part, odd_part * cosine + even_part * sine_part], axis=-1)
    return jnp.concatenate([rotated.reshape(rotary.shape), tensor[..., ROT:]], axis=-1)

def reference(hidden_in, norm_gain, norm_shift, attend_weight, output_weight, up_weight, up_bias, down_weight, down_bias, key_cache, value_cache, cached_len):
    score_scale = HD ** (-0.5)
    normed = layer_norm(hidden_in, norm_gain, norm_shift).astype(jnp.bfloat16)
    projected = jnp.dot(normed, attend_weight.reshape(D, 3 * HEADS * HD), preferred_element_type=jnp.float32)
    projected = projected.reshape(REQS, GROUP, 3, HEADS, HD)
    positions = cached_len[:, None] + jnp.arange(GROUP, dtype=jnp.int32)[None, :]
    queries = rotate_pairs(projected[:, :, 0], positions).astype(jnp.bfloat16)
    keys_new = rotate_pairs(projected[:, :, 1], positions).astype(jnp.bfloat16)
    values_new = projected[:, :, 2].astype(jnp.bfloat16)

    def one_request(packed):
        query_rows, fresh_keys, fresh_values, old_keys, old_values, length = packed
        old_keys = old_keys.reshape(CMAX, HEADS, HD).astype(jnp.float32)
        old_values = old_values.reshape(CMAX, HEADS, HD).astype(jnp.float32)
        query_float = query_rows.astype(jnp.float32)
        cache_scores = jnp.einsum('chd,phd->hcp', query_float, old_keys) * score_scale
        cache_scores = jnp.where(jnp.arange(CMAX, dtype=jnp.int32)[None, None, :] < length, cache_scores, -jnp.inf)
        group_scores = jnp.einsum('chd,khd->hck', query_float, fresh_keys.astype(jnp.float32)) * score_scale
        causal = jnp.arange(GROUP)[:, None] >= jnp.arange(GROUP)[None, :]
        group_scores = jnp.where(causal[None], group_scores, -jnp.inf)
        scores = jnp.concatenate([cache_scores, group_scores], axis=-1)
        top_score = lax.optimization_barrier(jnp.max(scores, axis=-1, keepdims=True))
        expo = jnp.exp(scores - top_score)
        weight_sum = lax.optimization_barrier(jnp.sum(expo, axis=-1))
        rounded = lax.optimization_barrier(expo.astype(jnp.bfloat16))
        weights = rounded.astype(jnp.float32)
        every_value = jnp.concatenate([old_values, fresh_values.astype(jnp.float32)], axis=0)
        context = jnp.einsum('hck,khd->chd', weights, every_value) / jnp.transpose(weight_sum)[:, :, None]
        return context.astype(jnp.bfloat16).reshape(GROUP, HEADS * HD)
    context = lax.map(one_request, (queries, keys_new, values_new, key_cache, value_cache, cached_len))
    context = context.reshape(TOKENS, HEADS * HD)
    attended = jnp.dot(context, output_weight, preferred_element_type=jnp.float32)
    upward = jnp.dot(normed, up_weight, preferred_element_type=jnp.float32) + up_bias
    active = jax.nn.gelu(upward, approximate=True).astype(jnp.bfloat16)
    downward = jnp.dot(active, down_weight, preferred_element_type=jnp.float32)
    hidden_out = (hidden_in.astype(jnp.float32) + (attended + downward) + down_bias).astype(jnp.bfloat16)
    return (hidden_out, keys_new.reshape(REQS, GROUP, HEADS * HD), values_new.reshape(REQS, GROUP, HEADS * HD))
```

```python
import functools

import jax
import jax.numpy as jnp
import numpy as np
from jax import lax
from jax.experimental import pallas as pl
from jax.experimental.pallas import tpu as pltpu
from jax.sharding import PartitionSpec as P

HD = 256
ROT = 64
GROUP = 128
D = 4096
TOK = 256
UNITS = 1024
SLOTS = 1536
Z = 8
COLS = D // Z
epsilon = 1e-05
very_low = -1e30
MESH = pl.DeviceIdType.MESH
F32 = jnp.float32
BF16 = jnp.bfloat16


def kernel(
    hid, gain, shift, wq, wo, wu, ub, wd, db, kc, vc, freq, lens,
    out, new_k, new_v,
    xg, nrm, wub, wdb, wqv, wov, kcv, vcv, gainv, shiftv, ubv, dbv, freqv,
    qbuf, kbuf, vbuf, ctx, act, part, rsend, rrecv,
    local_sem, zs, zr, ws, wr, ss, sr,
):
    r = lax.axis_index("req")
    z = lax.axis_index("head")
    core = r % 2
    y = (r // 2) % 4
    x = r // 8

    def device(c, a_, b_):
        x_ = (1 - c) * a_ + c * b_
        y_ = (1 - c) * b_ + c * a_
        return ((x_ % 4) * 4 + (y_ % 4)) * 2 + c

    a = (1 - core) * x + core * y
    b = (1 - core) * y + core * x
    partner = device(1 - core, b, a)
    a_plus, a_minus = device(core, a + 1, b), device(core, a + 3, b)
    b_plus, b_minus = device(core, a, b + 1), device(core, a, b + 3)
    z_plus, z_minus = (z + 1) % Z, (z + 7) % Z

    barrier = pltpu.get_barrier_semaphore()
    for who in (
        (a_plus, z), (a_minus, z), (b_plus, z), (b_minus, z), (partner, z),
        (r, z_plus), (r, z_minus),
    ):
        pl.semaphore_signal(barrier, inc=1, device_id=who, device_id_type=MESH)
    pl.semaphore_wait(barrier, 7)

    sent = []

    def remote(src, dst, send, recv, who):
        return pltpu.make_async_remote_copy(
            src_ref=src, dst_ref=dst, send_sem=send, recv_sem=recv,
            device_id=who, device_id_type=MESH,
        )

    def launch(src, dst, send, recv, who):
        copy = remote(src, dst, send, recv, who)
        copy.start()
        sent.append(copy)

    def zchunk(origin, c):
        return xg.at[origin, pl.ds(128 * c, 128), :]

    def zindex(direction, hop, c):
        return direction * 8 + (hop - 1) * 2 + c

    def zsend(direction, hop, c):
        origin = (z + Z - (hop - 1)) % Z if direction == 0 else (z + hop - 1) % Z
        src = hid.at[pl.ds(128 * c, 128), :] if hop == 1 else zchunk(origin, c)
        k = zindex(direction, hop, c)
        launch(src, zchunk(origin, c), zs.at[k], zr.at[k], (r, z_plus if direction == 0 else z_minus))

    def zwait(direction, hop, c):
        origin = (z + Z - hop) % Z if direction == 0 else (z + hop) % Z
        k = zindex(direction, hop, c)
        view = zchunk(origin, c)
        remote(view, view, zs.at[k], zr.at[k], (r, z_plus)).wait_recv()

    def zlast(direction, c):
        return 4 if c == direction else 3

    def zevent(direction, hop, c):
        zwait(direction, hop, c)
        if hop < zlast(direction, c):
            zsend(direction, hop + 1, c)

    own = (wu, wd)

    def slot(w, o):
        if w == 0:
            return wub.at[pl.ds(pl.multiple_of(o * 128, 128), 128), :]
        return wdb.at[o]

    def half(w, o, k):
        if w == 0:
            return wub.at[pl.ds(pl.multiple_of(o * 128 + 64 * k, 64), 64), :]
        return wdb.at[o, pl.ds(512 * k, 512), :]

    A_OF = (0, 3, 1, 2)

    def wsend(w, k, src, dst, who):
        launch(src, dst, ws.at[w, k], wr.at[w, k], (who, z))

    def wwait(w, k, view):
        remote(view, view, ws.at[w, k], wr.at[w, k], (partner, z)).wait_recv()

    def across(w, j, kb):
        o = device(core, a + A_OF[j], b + A_OF[kb])
        src = own[w] if j == 0 and kb == 0 else slot(w, o)
        wsend(w, 20 + 4 * j + kb, src, slot(w, o), partner)

    def second(w, j):
        o = device(core, a + A_OF[j], b)
        src = own[w] if j == 0 else slot(w, o)
        wsend(w, 4 + 4 * j, src, slot(w, o), b_plus)
        wsend(w, 5 + 4 * j, src, slot(w, o), b_minus)

    def start_own(w):
        wsend(w, 0, own[w], slot(w, r), a_plus)
        wsend(w, 1, own[w], slot(w, r), a_minus)
        second(w, 0)
        across(w, 0, 0)

    def first_event(w):
        o = device(core, a + 3, b)
        wwait(w, 0, slot(w, o))
        wsend(w, 2, half(w, o, 0), half(w, o, 0), a_plus)
        o = device(core, a + 1, b)
        wwait(w, 1, slot(w, o))
        wsend(w, 3, half(w, o, 1), half(w, o, 1), a_minus)
        second(w, 1)
        second(w, 2)
        across(w, 1, 0)
        across(w, 2, 0)

    def first_halves(w):
        o = device(core, a + 2, b)
        wwait(w, 2, half(w, o, 0))
        wwait(w, 3, half(w, o, 1))
        second(w, 3)
        across(w, 3, 0)

    def second_event(w, j):
        aj = a + A_OF[j]
        o = device(core, aj, b + 3)
        wwait(w, 4 + 4 * j, slot(w, o))
        wsend(w, 6 + 4 * j, half(w, o, 0), half(w, o, 0), b_plus)
        o = device(core, aj, b + 1)
        wwait(w, 5 + 4 * j, slot(w, o))
        wsend(w, 7 + 4 * j, half(w, o, 1), half(w, o, 1), b_minus)
        across(w, j, 1)
        across(w, j, 2)

    def second_halves(w, j):
        o = device(core, a + A_OF[j], b + 2)
        wwait(w, 6 + 4 * j, half(w, o, 0))
        wwait(w, 7 + 4 * j, half(w, o, 1))
        across(w, j, 3)

    def partner_waits(w):
        for j in range(4):
            for kb in range(4):
                o = device(1 - core, b + A_OF[j], a + A_OF[kb])
                wwait(w, 20 + 4 * j + kb, slot(w, o))

    locals_ = []

    def bring(src, dst):
        copy = pltpu.make_async_copy(src, dst, local_sem.at[len(locals_)])
        copy.start()
        locals_.append(copy)
        return copy

    for c in range(2):
        zsend(0, 1, c)
        zsend(1, 1, c)
    start_own(0)
    start_own(1)
    c_x = bring(hid, xg.at[z])
    c_small = [bring(gain, gainv), bring(shift, shiftv), bring(ub, ubv), bring(db, dbv), bring(freq, freqv)]
    c_u = bring(wu, slot(0, r))
    c_d = bring(wd, slot(1, r))
    c_q = bring(wq, wqv)
    c_k = bring(kc, kcv)
    c_v = bring(vc, vcv)
    c_o = bring(wo, wov)
    for copy in c_small:
        copy.wait()

    lane = lax.broadcasted_iota(jnp.int32, (TOK, 128), 1)
    row = lax.broadcasted_iota(jnp.int32, (TOK, 128), 0)
    position = jnp.where(row < GROUP, lens[0] + row, lens[1] + row - GROUP)
    angle = position.astype(F32) * freqv[...]
    cosine = jnp.cos(angle)
    sine = jnp.sin(angle)
    sine = jnp.where(lane % 2 == 0, -sine, sine)

    def rotate(t):
        head = t[:, :128]
        swapped = jnp.where(lane % 2 == 0, pltpu.roll(head, 127, 1), pltpu.roll(head, 1, 1))
        return jnp.concatenate([head * cosine + swapped * sine, t[:, 128:]], axis=1)

    zevent(0, 1, 0), zevent(1, 1, 0)
    first_event(0)
    second_event(0, 0)
    zevent(0, 1, 1), zevent(1, 1, 1)
    zevent(0, 2, 0), zevent(1, 2, 0)
    zevent(0, 2, 1), zevent(1, 2, 1)
    first_event(1)
    second_event(1, 0)
    zevent(0, 3, 0), zevent(1, 3, 0)
    first_halves(0)
    second_halves(0, 0)
    zevent(0, 3, 1), zevent(1, 3, 1)
    second_event(0, 1)
    second_event(0, 2)
    zevent(0, 4, 0), zevent(1, 4, 1)
    c_x.wait()

    @pl.loop(0, TOK // 16)
    def _(i):
        rows = pl.ds(pl.multiple_of(i * 16, 16), 16)
        total = jnp.zeros((16, 1), F32)
        for h in range(Z):
            total += jnp.sum(xg[h, rows, :].astype(F32), axis=1, keepdims=True)
        mean = total * (1.0 / D)
        square = jnp.zeros((16, 1), F32)
        for h in range(Z):
            center = xg[h, rows, :].astype(F32) - mean
            square += jnp.sum(center * center, axis=1, keepdims=True)
        scale = lax.rsqrt(square * (1.0 / D) + epsilon)
        for h in range(Z):
            cols = slice(h * COLS, (h + 1) * COLS)
            center = xg[h, rows, :].astype(F32) - mean
            nrm[rows, cols] = (center * scale * gainv[:, cols] + shiftv[:, cols]).astype(BF16)

    first_halves(1)
    second_halves(1, 0)
    second_event(0, 3)

    c_q.wait()
    qbuf[...] = rotate(jnp.dot(nrm[...], wqv[0], preferred_element_type=F32)).astype(BF16)
    second_halves(0, 1)
    second_halves(0, 2)
    kbuf[...] = rotate(jnp.dot(nrm[...], wqv[1], preferred_element_type=F32)).astype(BF16)
    vbuf[...] = jnp.dot(nrm[...], wqv[2], preferred_element_type=F32).astype(BF16)
    second_event(1, 1)
    second_event(1, 2)
    second_halves(0, 3)
    for q in range(2):
        new_k[q] = kbuf[pl.ds(q * GROUP, GROUP), :]
        new_v[q] = vbuf[pl.ds(q * GROUP, GROUP), :]

    c_k.wait()
    c_v.wait()
    nt = (((1,), (1,)), ((), ()))

    def attend(q):
        rows = pl.ds(q * GROUP, GROUP)
        query = qbuf[rows, :]
        old = lax.dot_general(query, kcv[q], nt, preferred_element_type=F32) * (HD ** -0.5)
        fresh = lax.dot_general(query, kbuf[rows, :], nt, preferred_element_type=F32) * (HD ** -0.5)
        place = lax.broadcasted_iota(jnp.int32, (GROUP, SLOTS), 1)
        old = jnp.where(place < lens[q], old, very_low)
        i0 = lax.broadcasted_iota(jnp.int32, (GROUP, GROUP), 0)
        i1 = lax.broadcasted_iota(jnp.int32, (GROUP, GROUP), 1)
        fresh = jnp.where(i1 <= i0, fresh, very_low)
        top = jnp.maximum(jnp.max(old, axis=1, keepdims=True), jnp.max(fresh, axis=1, keepdims=True))
        old = jnp.exp(old - top)
        fresh = jnp.exp(fresh - top)
        total = jnp.sum(old, axis=1, keepdims=True) + jnp.sum(fresh, axis=1, keepdims=True)
        mixed = jnp.dot(old.astype(BF16), vcv[q], preferred_element_type=F32)
        mixed += jnp.dot(fresh.astype(BF16), vbuf[rows, :], preferred_element_type=F32)
        ctx[rows, :] = (mixed / total).astype(BF16)

    attend(0)
    second_event(1, 3)
    attend(1)

    c_u.wait()
    partner_waits(0)

    @pl.loop(0, UNITS // 256)
    def _(n):
        cols = pl.ds(pl.multiple_of(n * 256, 256), 256)
        upward = jnp.dot(nrm[...], wub[:, cols], preferred_element_type=F32) + ubv[:, cols]
        act[:, cols] = jax.nn.gelu(upward, approximate=True).astype(BF16)

    second_halves(1, 1)
    second_halves(1, 2)
    second_halves(1, 3)
    c_d.wait()
    c_o.wait()
    partner_waits(1)

    def block(t):
        for i in range(2):
            weight = jnp.concatenate([wdb[4 * t + 2 * i], wdb[4 * t + 2 * i + 1]], axis=1)
            cols = pl.ds(pl.multiple_of(t * COLS + 256 * i, 256), 256)
            part[t, :, 256 * i:256 * (i + 1)] = jnp.dot(
                act[...], weight, preferred_element_type=F32
            ) + jnp.dot(ctx[...], wov[:, cols], preferred_element_type=F32)

    def rwait(direction, s, c):
        k = direction * 14 + 2 * s + c
        view = rrecv.at[direction, s, pl.ds(64 * c, 64), :]
        remote(view, view, ss.at[k], sr.at[k], (r, z_plus)).wait_recv()

    block((z + 7) % Z)
    for s in range(7):
        for direction in range(2):
            if s < 3 and direction == 1:
                block((z + 1 + s) % Z)
            t = (z + 7 - s) % Z if direction == 0 else (z + 1 + s) % Z
            for c in range(2):
                rows = pl.ds(128 * direction + 64 * c, 64)
                inner = pl.ds(64 * c, 64)
                value = part[t, rows, :]
                if s > 0:
                    rwait(direction, s - 1, c)
                    value += rrecv[direction, s - 1, inner, :].astype(F32)
                rsend[direction, s, inner, :] = value.astype(BF16)
                k = direction * 14 + 2 * s + c
                launch(
                    rsend.at[direction, s, inner, :], rrecv.at[direction, s, inner, :],
                    ss.at[k], sr.at[k], (r, z_plus if direction == 0 else z_minus),
                )
        if s < 3:
            block((z + 6 - s) % Z)
        if s == 3:
            block(z)
    for direction in range(2):
        for c in range(2):
            rows = pl.ds(128 * direction + 64 * c, 64)
            inner = pl.ds(64 * c, 64)
            rwait(direction, 6, c)
            value = part[z, rows, :] + rrecv[direction, 6, inner, :].astype(F32)
            out[rows, :] = (xg[z, rows, :].astype(F32) + value + dbv[...]).astype(BF16)
    for copy in sent:
        copy.wait_send()


def body(
    hidden_in, norm_gain, norm_shift, attend_weight, output_weight, up_weight,
    up_bias, down_weight, down_bias, key_cache, value_cache, cached_len,
):
    lanes = np.arange(128)
    freq = np.where(lanes < ROT, 10000.0 ** (-(2.0 * (lanes // 2)) / ROT), 0.0)
    freq = jnp.asarray(freq[None, :], dtype=F32)
    anywhere = pl.BlockSpec(memory_space=pl.ANY)
    vmem = pl.BlockSpec(memory_space=pltpu.VMEM)
    dma = pltpu.SemaphoreType.DMA
    return pl.pallas_call(
        kernel,
        out_shape=(
            jax.ShapeDtypeStruct((TOK, COLS), BF16),
            jax.ShapeDtypeStruct((2, GROUP, HD), BF16),
            jax.ShapeDtypeStruct((2, GROUP, HD), BF16),
        ),
        in_specs=[anywhere] * 12 + [pl.BlockSpec(memory_space=pltpu.SMEM)],
        out_specs=(vmem, vmem, vmem),
        scratch_shapes=[
            pltpu.VMEM((Z, TOK, COLS), BF16),
            pltpu.VMEM((TOK, D), BF16),
            pltpu.VMEM((D, UNITS), BF16),
            pltpu.VMEM((32, UNITS, 128), BF16),
            pltpu.VMEM((3, D, HD), BF16),
            pltpu.VMEM((HD, D), BF16),
            pltpu.VMEM((2, SLOTS, HD), BF16),
            pltpu.VMEM((2, SLOTS, HD), BF16),
            pltpu.VMEM((1, D), F32),
            pltpu.VMEM((1, D), F32),
            pltpu.VMEM((1, UNITS), F32),
            pltpu.VMEM((1, COLS), F32),
            pltpu.VMEM((1, 128), F32),
            pltpu.VMEM((TOK, HD), BF16),
            pltpu.VMEM((TOK, HD), BF16),
            pltpu.VMEM((TOK, HD), BF16),
            pltpu.VMEM((TOK, HD), BF16),
            pltpu.VMEM((TOK, UNITS), BF16),
            pltpu.VMEM((Z, TOK, COLS), F32),
            pltpu.VMEM((2, 7, 128, COLS), BF16),
            pltpu.VMEM((2, 7, 128, COLS), BF16),
            dma((12,)),
            dma((16,)),
            dma((16,)),
            dma((2, 36)),
            dma((2, 36)),
            dma((28,)),
            dma((28,)),
        ],
        compiler_params=pltpu.CompilerParams(
            collective_id=0, has_side_effects=True, vmem_limit_bytes=66 * 1000 * 1000
        ),
    )(
        hidden_in, norm_gain[None, :], norm_shift[None, :],
        jnp.transpose(attend_weight, (1, 0, 2)), output_weight, up_weight,
        up_bias[None, :], down_weight, down_bias[None, :], key_cache, value_cache, freq, cached_len,
    )


def solution(mesh):
    placed = (
        P("req", "head"), P(), P(), P(None, None, "head"), P("head", None), P("req", "head"),
        P("head"), P("head", "req"), P("head"), P("req", None, "head"), P("req", None, "head"), P("req"),
    )
    return jax.shard_map(
        body,
        mesh=mesh,
        in_specs=placed,
        out_specs=(P("req", "head"), P("req", None, "head"), P("req", None, "head")),
        check_vma=False,
    )
```

```python
import functools

import jax
import jax.numpy as jnp
import numpy as np
from jax import lax
from jax.experimental import pallas as pl
from jax.experimental.pallas import tpu as pltpu
from jax.sharding import PartitionSpec as P

HD = 256
ROT = 64
GROUP = 128
D = 4096
TOK = 256
UNITS = 1024
SLOTS = 1536
Z = 8
COLS = D // Z
epsilon = 1e-05
very_low = -1e30
PIECES = 4
MESH = pl.DeviceIdType.MESH
F32 = jnp.float32
BF16 = jnp.bfloat16


def kernel(
    hid, gain, shift, wq, wo, wu, ub, wd, db, kc, vc, freq, lens_in,
    out, new_k, new_v,
    xg, nrm, wub, wdb, wqv, wov, kcv, vcv, gainv, shiftv, ubv, dbv, freqv,
    qbuf, kbuf, vbuf, ctx, act, part, rsend, rrecv, lens,
    local_sem, zs, zr, ws, wr, ss, sr,
):
    r = lax.axis_index("req")
    z = lax.axis_index("head")
    core = r % 2
    y = (r // 2) % 4
    x = r // 8

    def device(c, a_, b_):
        x_ = (1 - c) * a_ + c * b_
        y_ = (1 - c) * b_ + c * a_
        return ((x_ % 4) * 4 + (y_ % 4)) * 2 + c

    a = (1 - core) * x + core * y
    b = (1 - core) * y + core * x
    partner = device(1 - core, b, a)
    a_plus, a_minus = device(core, a + 1, b), device(core, a + 3, b)
    b_plus, b_minus = device(core, a, b + 1), device(core, a, b + 3)
    z_plus, z_minus = (z + 1) % Z, (z + 7) % Z

    barrier = pltpu.get_barrier_semaphore()
    for who in (
        (a_plus, z), (a_minus, z), (b_plus, z), (b_minus, z), (partner, z),
        (r, z_plus), (r, z_minus),
    ):
        pl.semaphore_signal(barrier, inc=1, device_id=who, device_id_type=MESH)
    pl.semaphore_wait(barrier, 7)

    sent = []

    def remote(src, dst, send, recv, who):
        return pltpu.make_async_remote_copy(
            src_ref=src, dst_ref=dst, send_sem=send, recv_sem=recv,
            device_id=who, device_id_type=MESH,
        )

    def launch(src, dst, send, recv, who):
        copy = remote(src, dst, send, recv, who)
        copy.start()
        sent.append(copy)

    def zchunk(origin, c):
        return xg.at[origin, pl.ds(128 * c, 128), :]

    def zindex(direction, hop, c):
        return direction * 8 + (hop - 1) * 2 + c

    def zsend(direction, hop, c):
        origin = (z + Z - (hop - 1)) % Z if direction == 0 else (z + hop - 1) % Z
        src = hid.at[pl.ds(128 * c, 128), :] if hop == 1 else zchunk(origin, c)
        k = zindex(direction, hop, c)
        launch(src, zchunk(origin, c), zs.at[k], zr.at[k], (r, z_plus if direction == 0 else z_minus))

    def zwait(direction, hop, c):
        origin = (z + Z - hop) % Z if direction == 0 else (z + hop) % Z
        k = zindex(direction, hop, c)
        view = zchunk(origin, c)
        remote(view, view, zs.at[k], zr.at[k], (r, z_plus)).wait_recv()

    def zlast(direction, c):
        return 4 if c == direction else 3

    def zevent(direction, hop, c):
        zwait(direction, hop, c)
        if hop < zlast(direction, c):
            zsend(direction, hop + 1, c)

    own = (wu, wd)

    def slot(w, o):
        if w == 0:
            return wub.at[pl.ds(pl.multiple_of(o * 128, 128), 128), :]
        return wdb.at[o]

    def half(w, o, k):
        if w == 0:
            return wub.at[pl.ds(pl.multiple_of(o * 128 + 64 * k, 64), 64), :]
        return wdb.at[o, pl.ds(512 * k, 512), :]

    A_OF = (0, 3, 1, 2)

    def wsend(w, k, src, dst, who):
        launch(src, dst, ws.at[w, k], wr.at[w, k], (who, z))

    def wwait(w, k, view):
        remote(view, view, ws.at[w, k], wr.at[w, k], (partner, z)).wait_recv()

    def across(w, j, kb):
        o = device(core, a + A_OF[j], b + A_OF[kb])
        src = own[w] if j == 0 and kb == 0 else slot(w, o)
        wsend(w, 20 + 4 * j + kb, src, slot(w, o), partner)

    def second(w, j):
        o = device(core, a + A_OF[j], b)
        src = own[w] if j == 0 else slot(w, o)
        wsend(w, 4 + 4 * j, src, slot(w, o), b_plus)
        wsend(w, 5 + 4 * j, src, slot(w, o), b_minus)

    def start_own(w):
        wsend(w, 0, own[w], slot(w, r), a_plus)
        wsend(w, 1, own[w], slot(w, r), a_minus)
        second(w, 0)
        across(w, 0, 0)

    def first_event(w):
        o = device(core, a + 3, b)
        wwait(w, 0, slot(w, o))
        wsend(w, 2, half(w, o, 0), half(w, o, 0), a_plus)
        o = device(core, a + 1, b)
        wwait(w, 1, slot(w, o))
        wsend(w, 3, half(w, o, 1), half(w, o, 1), a_minus)
        second(w, 1)
        second(w, 2)
        across(w, 1, 0)
        across(w, 2, 0)

    def first_halves(w):
        o = device(core, a + 2, b)
        wwait(w, 2, half(w, o, 0))
        wwait(w, 3, half(w, o, 1))
        second(w, 3)
        across(w, 3, 0)

    def second_event(w, j):
        aj = a + A_OF[j]
        o = device(core, aj, b + 3)
        wwait(w, 4 + 4 * j, slot(w, o))
        wsend(w, 6 + 4 * j, half(w, o, 0), half(w, o, 0), b_plus)
        o = device(core, aj, b + 1)
        wwait(w, 5 + 4 * j, slot(w, o))
        wsend(w, 7 + 4 * j, half(w, o, 1), half(w, o, 1), b_minus)
        across(w, j, 1)
        across(w, j, 2)

    def second_halves(w, j):
        o = device(core, a + A_OF[j], b + 2)
        wwait(w, 6 + 4 * j, half(w, o, 0))
        wwait(w, 7 + 4 * j, half(w, o, 1))
        across(w, j, 3)

    def partner_waits(w):
        for j in range(4):
            for kb in range(4):
                o = device(1 - core, b + A_OF[j], a + A_OF[kb])
                wwait(w, 20 + 4 * j + kb, slot(w, o))

    locals_ = []

    def bring(src, dst):
        copy = pltpu.make_async_copy(src, dst, local_sem.at[len(locals_)])
        copy.start()
        locals_.append(copy)
        return copy

    for c in range(2):
        zsend(0, 1, c)
        zsend(1, 1, c)
    start_own(0)
    start_own(1)
    c_x = bring(hid, xg.at[z])
    c_small = [bring(lens_in, lens), bring(gain, gainv), bring(shift, shiftv), bring(ub, ubv), bring(db, dbv), bring(freq, freqv)]
    c_u = bring(wu, slot(0, r))
    c_d = bring(wd, slot(1, r))
    c_q = bring(wq, wqv)
    c_k = bring(kc, kcv)
    c_v = bring(vc, vcv)
    c_o = bring(wo, wov)
    for copy in c_small:
        copy.wait()

    lane = lax.broadcasted_iota(jnp.int32, (TOK, 128), 1)
    turn = [lens[q].astype(F32) * freqv[pl.ds(0, 8), :] for q in range(2)]

    def rotation():
        cosines, sines = [], []
        for q in range(2):
            cl, sl = jnp.cos(turn[q])[:1], jnp.sin(turn[q])[:1]
            ct, st = freqv[pl.ds(8, GROUP), :], freqv[pl.ds(8 + GROUP, GROUP), :]
            cosines.append(cl * ct - sl * st)
            sines.append(sl * ct + cl * st)
        cosine = jnp.concatenate(cosines, axis=0)
        sine = jnp.concatenate(sines, axis=0)
        return cosine, jnp.where(lane % 2 == 0, -sine, sine)

    def rotate(t):
        head = t[:, :128]
        swapped = jnp.where(lane % 2 == 0, pltpu.roll(head, 127, 1), pltpu.roll(head, 1, 1))
        return jnp.concatenate([head * cosine + swapped * sine, t[:, 128:]], axis=1)

    zevent(0, 1, 0), zevent(1, 1, 0)
    first_event(0)
    second_event(0, 0)
    zevent(0, 1, 1), zevent(1, 1, 1)
    zevent(0, 2, 0), zevent(1, 2, 0)
    zevent(0, 2, 1), zevent(1, 2, 1)
    first_event(1)
    second_event(1, 0)
    zevent(0, 3, 0), zevent(1, 3, 0)
    first_halves(0)
    second_halves(0, 0)
    zevent(0, 3, 1), zevent(1, 3, 1)
    second_event(0, 1)
    second_event(0, 2)
    zevent(0, 4, 0), zevent(1, 4, 1)
    c_x.wait()

    @pl.loop(0, TOK // 16)
    def _(i):
        rows = pl.ds(pl.multiple_of(i * 16, 16), 16)
        total = jnp.zeros((16, 1), F32)
        for h in range(Z):
            total += jnp.sum(xg[h, rows, :].astype(F32), axis=1, keepdims=True)
        mean = total * (1.0 / D)
        square = jnp.zeros((16, 1), F32)
        for h in range(Z):
            center = xg[h, rows, :].astype(F32) - mean
            square += jnp.sum(center * center, axis=1, keepdims=True)
        scale = lax.rsqrt(square * (1.0 / D) + epsilon)
        for h in range(Z):
            cols = slice(h * COLS, (h + 1) * COLS)
            center = xg[h, rows, :].astype(F32) - mean
            nrm[rows, cols] = (center * scale * gainv[:, cols] + shiftv[:, cols]).astype(BF16)

    first_halves(1)
    second_halves(1, 0)
    second_event(0, 3)

    cosine, sine = rotation()
    c_q.wait()
    qbuf[...] = rotate(jnp.dot(nrm[...], wqv[0], preferred_element_type=F32)).astype(BF16)
    second_halves(0, 1)
    second_halves(0, 2)
    kbuf[...] = rotate(jnp.dot(nrm[...], wqv[1], preferred_element_type=F32)).astype(BF16)
    vbuf[...] = jnp.dot(nrm[...], wqv[2], preferred_element_type=F32).astype(BF16)
    second_event(1, 1)
    second_event(1, 2)
    second_halves(0, 3)
    for q in range(2):
        new_k[q] = kbuf[pl.ds(q * GROUP, GROUP), :]
        new_v[q] = vbuf[pl.ds(q * GROUP, GROUP), :]

    c_k.wait()
    c_v.wait()
    nt = (((1,), (1,)), ((), ()))

    def attend(q):
        rows = pl.ds(q * GROUP, GROUP)
        query = qbuf[rows, :]
        old = lax.dot_general(query, kcv[q], nt, preferred_element_type=F32) * (HD ** -0.5)
        fresh = lax.dot_general(query, kbuf[rows, :], nt, preferred_element_type=F32) * (HD ** -0.5)
        place = lax.broadcasted_iota(jnp.int32, (GROUP, SLOTS), 1)
        old = jnp.where(place < lens[q], old, very_low)
        i0 = lax.broadcasted_iota(jnp.int32, (GROUP, GROUP), 0)
        i1 = lax.broadcasted_iota(jnp.int32, (GROUP, GROUP), 1)
        fresh = jnp.where(i1 <= i0, fresh, very_low)
        top = jnp.maximum(jnp.max(old, axis=1, keepdims=True), jnp.max(fresh, axis=1, keepdims=True))
        old = jnp.exp(old - top)
        fresh = jnp.exp(fresh - top)
        total = jnp.sum(old, axis=1, keepdims=True) + jnp.sum(fresh, axis=1, keepdims=True)
        mixed = jnp.dot(old.astype(BF16), vcv[q], preferred_element_type=F32)
        mixed += jnp.dot(fresh.astype(BF16), vbuf[rows, :], preferred_element_type=F32)
        ctx[rows, :] = (mixed / total).astype(BF16)

    attend(0)
    second_event(1, 3)
    attend(1)

    c_u.wait()
    partner_waits(0)

    @pl.loop(0, UNITS // 256)
    def _(n):
        cols = pl.ds(pl.multiple_of(n * 256, 256), 256)
        upward = jnp.dot(nrm[...], wub[:, cols], preferred_element_type=F32) + ubv[:, cols]
        act[:, cols] = jax.nn.gelu(upward, approximate=True).astype(BF16)

    second_halves(1, 1)
    second_halves(1, 2)
    second_halves(1, 3)
    c_d.wait()
    c_o.wait()
    partner_waits(1)

    def block(t):
        for i in range(2):
            weight = jnp.concatenate([wdb[4 * t + 2 * i], wdb[4 * t + 2 * i + 1]], axis=1)
            cols = pl.ds(pl.multiple_of(t * COLS + 256 * i, 256), 256)
            part[t, :, 256 * i:256 * (i + 1)] = jnp.dot(
                act[...], weight, preferred_element_type=F32
            ) + jnp.dot(ctx[...], wov[:, cols], preferred_element_type=F32)

    piece = GROUP // PIECES

    def rwait(direction, s, c):
        k = (direction * 7 + s) * PIECES + c
        view = rrecv.at[direction, s, pl.ds(piece * c, piece), :]
        remote(view, view, ss.at[k], sr.at[k], (r, z_plus)).wait_recv()

    def hand_on(direction, s):
        t = (z + 7 - s) % Z if direction == 0 else (z + 1 + s) % Z
        for c in range(PIECES):
            rows = pl.ds(128 * direction + piece * c, piece)
            inner = pl.ds(piece * c, piece)
            value = part[t, rows, :]
            if s > 0:
                rwait(direction, s - 1, c)
                value += rrecv[direction, s - 1, inner, :].astype(F32)
            rsend[direction, s, inner, :] = value.astype(BF16)
            k = (direction * 7 + s) * PIECES + c
            launch(
                rsend.at[direction, s, inner, :], rrecv.at[direction, s, inner, :],
                ss.at[k], sr.at[k], (r, z_plus if direction == 0 else z_minus),
            )

    block((z + 7) % Z)
    hand_on(0, 0)
    block((z + 1) % Z)
    hand_on(1, 0)
    for s in range(1, 7):
        if s < 3:
            block((z + 7 - s) % Z)
            block((z + 1 + s) % Z)
        elif s == 3:
            block((z + 4) % Z)
        elif s == 4:
            block(z)
        hand_on(0, s)
        hand_on(1, s)
    for c in range(PIECES):
        for direction in range(2):
            rows = pl.ds(128 * direction + piece * c, piece)
            inner = pl.ds(piece * c, piece)
            rwait(direction, 6, c)
            value = part[z, rows, :] + rrecv[direction, 6, inner, :].astype(F32)
            out[rows, :] = (xg[z, rows, :].astype(F32) + value + dbv[...]).astype(BF16)
    for copy in sent:
        copy.wait_send()


def body(
    hidden_in, norm_gain, norm_shift, attend_weight, output_weight, up_weight,
    up_bias, down_weight, down_bias, key_cache, value_cache, cached_len,
):
    lanes = np.arange(128)
    freq = np.where(lanes < ROT, 10000.0 ** (-(2.0 * (lanes // 2)) / ROT), 0.0)
    steps = np.arange(GROUP)[:, None] * freq[None, :]
    tables = np.concatenate([np.tile(freq, (8, 1)), np.cos(steps), np.sin(steps)], axis=0)
    freq = jnp.asarray(tables, dtype=F32)
    anywhere = pl.BlockSpec(memory_space=pltpu.HBM)
    vmem = pl.BlockSpec(memory_space=pltpu.VMEM)
    dma = pltpu.SemaphoreType.DMA
    return pl.pallas_call(
        kernel,
        out_shape=(
            jax.ShapeDtypeStruct((TOK, COLS), BF16),
            jax.ShapeDtypeStruct((2, GROUP, HD), BF16),
            jax.ShapeDtypeStruct((2, GROUP, HD), BF16),
        ),
        in_specs=[anywhere] * 13,
        out_specs=(vmem, vmem, vmem),
        scratch_shapes=[
            pltpu.VMEM((Z, TOK, COLS), BF16),
            pltpu.VMEM((TOK, D), BF16),
            pltpu.VMEM((D, UNITS), BF16),
            pltpu.VMEM((32, UNITS, 128), BF16),
            pltpu.VMEM((3, D, HD), BF16),
            pltpu.VMEM((HD, D), BF16),
            pltpu.VMEM((2, SLOTS, HD), BF16),
            pltpu.VMEM((2, SLOTS, HD), BF16),
            pltpu.VMEM((1, D), F32),
            pltpu.VMEM((1, D), F32),
            pltpu.VMEM((1, UNITS), F32),
            pltpu.VMEM((1, COLS), F32),
            pltpu.VMEM((8 + 2 * GROUP, 128), F32),
            pltpu.VMEM((TOK, HD), BF16),
            pltpu.VMEM((TOK, HD), BF16),
            pltpu.VMEM((TOK, HD), BF16),
            pltpu.VMEM((TOK, HD), BF16),
            pltpu.VMEM((TOK, UNITS), BF16),
            pltpu.VMEM((Z, TOK, COLS), F32),
            pltpu.VMEM((2, 7, 128, COLS), BF16),
            pltpu.VMEM((2, 7, 128, COLS), BF16),
            pltpu.SMEM((2,), jnp.int32),
            dma((13,)),
            dma((16,)),
            dma((16,)),
            dma((2, 36)),
            dma((2, 36)),
            dma((14 * PIECES,)),
            dma((14 * PIECES,)),
        ],
        compiler_params=pltpu.CompilerParams(
            collective_id=0, has_side_effects=True, vmem_limit_bytes=50 * 1000 * 1000
        ),
    )(
        *[
            pltpu.with_memory_space_constraint(v, pltpu.HBM)
            for v in (
                hidden_in, norm_gain[None, :], norm_shift[None, :],
                jnp.transpose(attend_weight, (1, 0, 2)), output_weight, up_weight,
                up_bias[None, :], down_weight, down_bias[None, :], key_cache, value_cache, freq,
                cached_len,
            )
        ]
    )


def solution(mesh):
    placed = (
        P("req", "head"), P(), P(), P(None, None, "head"), P("head", None), P("req", "head"),
        P("head"), P("head", "req"), P("head"), P("req", None, "head"), P("req", None, "head"), P("req"),
    )
    return jax.shard_map(
        body,
        mesh=mesh,
        in_specs=placed,
        out_specs=(P("req", "head"), P("req", None, "head"), P("req", None, "head")),
        check_vma=False,
    )
```

```python
import functools

import jax
import jax.numpy as jnp
import numpy as np
from jax import lax
from jax.experimental import pallas as pl
from jax.experimental.pallas import tpu as pltpu
from jax.sharding import PartitionSpec as P

HD = 256
ROT = 64
GROUP = 128
D = 4096
TOK = 256
UNITS = 1024
SLOTS = 1536
Z = 8
COLS = D // Z
epsilon = 1e-05
very_low = -1e30
ORDER = (
    ("Z", 1, 0), ("F", 0), ("Z", 1, 1), ("Z", 2, 0), ("Z", 2, 1), ("F", 1), ("S", 0, 0), ("Z", 3, 0),
    ("S", 0, 2), ("Z", 3, 1), ("H", 1), ("H", 0), ("S", 0, 1), ("Z", 4, 1), ("Z", 4, 0), ("ln", 0),
    ("S", 1, 1), ("T", 0, 0), ("ln", 1), ("project", 2), ("project", 1), ("S", 0, 3), ("S", 1, 2), ("S", 1, 3),
    ("project", 0), ("at", 1), ("T", 0, 2), ("T", 0, 1), ("S", 1, 0), ("own", 2), ("T", 0, 3), ("at", 0),
    ("T", 1, 1), ("P", 0), ("up", 3), ("up", 0), ("F", 2), ("T", 1, 2), ("T", 1, 3), ("T", 1, 0),
    ("up", 2), ("up", 1), ("P", 1), ("B", 0, 0), ("N", 0, 0), ("H", 2), ("B", 0, 2), ("S", 2, 0),
    ("B", 0, 1), ("S", 2, 1), ("N", 0, 1), ("S", 2, 2), ("S", 2, 3), ("B", 0, 3), ("T", 2, 2), ("T", 2, 1),
    ("T", 2, 0), ("N", 0, 2), ("T", 2, 3), ("P", 2), ("B", 1, 0), ("N", 1, 0), ("N", 0, 3), ("B", 1, 1),
    ("N", 1, 1), ("B", 0, 4), ("B", 1, 4), ("B", 1, 3), ("E", 0), ("B", 1, 2), ("N", 1, 2), ("N", 1, 3),
    ("E", 1),
)
MESH = pl.DeviceIdType.MESH
F32 = jnp.float32
BF16 = jnp.bfloat16


def kernel(
    hid, gain, shift, wq, wo, wu, ub, wd, db, kc, vc, freq, lens_in,
    out, new_k, new_v,
    xg, nrm, wub, wdb, wqv, wov, kcv, vcv, gainv, shiftv, ubv, dbv, freqv,
    qbuf, kbuf, vbuf, ctx, act, part, rsend, rrecv, lens,
    local_sem, zs, zr, ws, wr, ss, sr, xs, xr,
):
    r = lax.axis_index("req")
    z = lax.axis_index("head")
    core = r % 2
    y = (r // 2) % 4
    x = r // 8

    def device(c, a_, b_):
        x_ = (1 - c) * a_ + c * b_
        y_ = (1 - c) * b_ + c * a_
        return ((x_ % 4) * 4 + (y_ % 4)) * 2 + c

    a = (1 - core) * x + core * y
    b = (1 - core) * y + core * x
    partner = device(1 - core, b, a)
    a_plus, a_minus = device(core, a + 1, b), device(core, a + 3, b)
    b_plus, b_minus = device(core, a, b + 1), device(core, a, b + 3)
    z_plus, z_minus = (z + 1) % Z, (z + 7) % Z

    barrier = pltpu.get_barrier_semaphore()
    for who in (
        (a_plus, z), (a_minus, z), (b_plus, z), (b_minus, z), (partner, z),
        (r, z_plus), (r, z_minus),
    ):
        pl.semaphore_signal(barrier, inc=1, device_id=who, device_id_type=MESH)
    pl.semaphore_wait(barrier, 7)

    sent = []

    def remote(src, dst, send, recv, who):
        return pltpu.make_async_remote_copy(
            src_ref=src, dst_ref=dst, send_sem=send, recv_sem=recv,
            device_id=who, device_id_type=MESH,
        )

    def launch(src, dst, send, recv, who):
        copy = remote(src, dst, send, recv, who)
        copy.start()
        sent.append(copy)

    def zchunk(origin, c):
        return xg.at[origin, pl.ds(128 * c, 128), :]

    def zindex(direction, hop, c):
        return direction * 8 + (hop - 1) * 2 + c

    def zsend(direction, hop, c):
        origin = (z + Z - (hop - 1)) % Z if direction == 0 else (z + hop - 1) % Z
        src = hid.at[pl.ds(128 * c, 128), :] if hop == 1 else zchunk(origin, c)
        k = zindex(direction, hop, c)
        launch(src, zchunk(origin, c), zs.at[k], zr.at[k], (r, z_plus if direction == 0 else z_minus))

    def zwait(direction, hop, c):
        origin = (z + Z - hop) % Z if direction == 0 else (z + hop) % Z
        k = zindex(direction, hop, c)
        view = zchunk(origin, c)
        remote(view, view, zs.at[k], zr.at[k], (r, z_plus)).wait_recv()

    def zlast(direction, c):
        return 4 if c == direction else 3

    def zevent(direction, hop, c):
        zwait(direction, hop, c)
        if hop < zlast(direction, c):
            zsend(direction, hop + 1, c)

    def slot(w, o):
        if w == 0:
            return wub.at[pl.ds(pl.multiple_of(o * 128, 128), 128), :]
        return wdb.at[(o // 2) * 2 + w - 1, pl.ds(pl.multiple_of((o % 2) * 512, 512), 512), :]

    def half(w, o, k):
        if w == 0:
            return wub.at[pl.ds(pl.multiple_of(o * 128 + 64 * k, 64), 64), :]
        return wdb.at[(o // 2) * 2 + w - 1, pl.ds(pl.multiple_of((o % 2) * 512 + 256 * k, 256), 256), :]

    A_OF = (0, 3, 1, 2)

    def wsend(w, k, src, dst, who):
        launch(src, dst, ws.at[w, k], wr.at[w, k], (who, z))

    def wwait(w, k, view):
        remote(view, view, ws.at[w, k], wr.at[w, k], (partner, z)).wait_recv()

    def across(w, j, kb):
        o = device(core, a + A_OF[j], b + A_OF[kb])
        src = wu if w == 0 and j == 0 and kb == 0 else slot(w, o)
        wsend(w, 20 + 4 * j + kb, src, slot(w, o), partner)

    def second(w, j):
        o = device(core, a + A_OF[j], b)
        src = wu if w == 0 and j == 0 else slot(w, o)
        wsend(w, 4 + 4 * j, src, slot(w, o), b_plus)
        wsend(w, 5 + 4 * j, src, slot(w, o), b_minus)

    def start_own(w):
        src = wu if w == 0 else slot(w, r)
        wsend(w, 0, src, slot(w, r), a_plus)
        wsend(w, 1, src, slot(w, r), a_minus)
        second(w, 0)
        if w == 0:
            across(w, 0, 0)

    def first_event(w):
        o = device(core, a + 3, b)
        wwait(w, 0, slot(w, o))
        wsend(w, 2, half(w, o, 0), half(w, o, 0), a_plus)
        o = device(core, a + 1, b)
        wwait(w, 1, slot(w, o))
        wsend(w, 3, half(w, o, 1), half(w, o, 1), a_minus)
        second(w, 1)
        second(w, 2)
        across(w, 1, 0)
        across(w, 2, 0)

    def first_halves(w):
        o = device(core, a + 2, b)
        wwait(w, 2, half(w, o, 0))
        wwait(w, 3, half(w, o, 1))
        second(w, 3)
        across(w, 3, 0)

    def second_event(w, j):
        aj = a + A_OF[j]
        o = device(core, aj, b + 3)
        wwait(w, 4 + 4 * j, slot(w, o))
        wsend(w, 6 + 4 * j, half(w, o, 0), half(w, o, 0), b_plus)
        o = device(core, aj, b + 1)
        wwait(w, 5 + 4 * j, slot(w, o))
        wsend(w, 7 + 4 * j, half(w, o, 1), half(w, o, 1), b_minus)
        across(w, j, 1)
        across(w, j, 2)

    def second_halves(w, j):
        o = device(core, a + A_OF[j], b + 2)
        wwait(w, 6 + 4 * j, half(w, o, 0))
        wwait(w, 7 + 4 * j, half(w, o, 1))
        across(w, j, 3)

    def partner_waits(w):
        for j in range(4):
            for kb in range(4):
                if w > 0 and j == 0 and kb == 0:
                    continue
                o = device(1 - core, b + A_OF[j], a + A_OF[kb])
                wwait(w, 20 + 4 * j + kb, slot(w, o))

    locals_ = []
    pending = {}

    def need(*names):
        for name in names:
            if name in pending:
                pending.pop(name).wait()

    def bring(src, dst):
        copy = pltpu.make_async_copy(src, dst, local_sem.at[len(locals_)])
        copy.start()
        locals_.append(copy)
        return copy

    for c in range(2):
        zsend(0, 1, c)
        zsend(1, 1, c)
    start_own(0)
    launch(wd, wdb.at[r], xs.at[0], xr.at[0], (partner, z))
    c_d = bring(wd, wdb.at[r])
    pending["x"] = bring(hid, xg.at[z])
    c_small = [bring(lens_in, lens), bring(gain, gainv), bring(shift, shiftv), bring(ub, ubv), bring(db, dbv), bring(freq, freqv)]
    pending["u"] = bring(wu, slot(0, r))
    pending["q"] = bring(wq, wqv)
    pending["k"] = bring(kc, kcv)
    pending["v"] = bring(vc, vcv)
    pending["o"] = bring(wo, wov)
    for copy in c_small:
        copy.wait()
    c_d.wait()
    remote(wdb.at[partner], wdb.at[partner], xs.at[0], xr.at[0], (partner, z)).wait_recv()
    start_own(1)

    lane = lax.broadcasted_iota(jnp.int32, (TOK, 128), 1)
    turn = [lens[q].astype(F32) * freqv[pl.ds(0, 8), :] for q in range(2)]

    def rotation():
        cosines, sines = [], []
        for q in range(2):
            cl, sl = jnp.cos(turn[q])[:1], jnp.sin(turn[q])[:1]
            ct, st = freqv[pl.ds(8, GROUP), :], freqv[pl.ds(8 + GROUP, GROUP), :]
            cosines.append(cl * ct - sl * st)
            sines.append(sl * ct + cl * st)
        cosine = jnp.concatenate(cosines, axis=0)
        sine = jnp.concatenate(sines, axis=0)
        return cosine, jnp.where(lane % 2 == 0, -sine, sine)

    def rotate(t, cosine, sine):
        head = t[:, :128]
        swapped = jnp.where(lane % 2 == 0, pltpu.roll(head, 127, 1), pltpu.roll(head, 1, 1))
        return jnp.concatenate([head * cosine + swapped * sine, t[:, 128:]], axis=1)

    def norm(n):
        need("x")

        @pl.loop(n * 8, n * 8 + 8)
        def _(i):
            rows = pl.ds(pl.multiple_of(i * 16, 16), 16)
            total = jnp.zeros((16, 1), F32)
            for h in range(Z):
                total += jnp.sum(xg[h, rows, :].astype(F32), axis=1, keepdims=True)
            mean = total * (1.0 / D)
            square = jnp.zeros((16, 1), F32)
            for h in range(Z):
                center = xg[h, rows, :].astype(F32) - mean
                square += jnp.sum(center * center, axis=1, keepdims=True)
            scale = lax.rsqrt(square * (1.0 / D) + epsilon)
            for h in range(Z):
                cols = slice(h * COLS, (h + 1) * COLS)
                center = xg[h, rows, :].astype(F32) - mean
                nrm[rows, cols] = (center * scale * gainv[:, cols] + shiftv[:, cols]).astype(BF16)

    def project(n):
        need("q")
        value = jnp.dot(nrm[...], wqv[n], preferred_element_type=F32)
        if n < 2:
            value = rotate(value, *rotation())
        buffer = (qbuf, kbuf, vbuf)[n]
        buffer[...] = value.astype(BF16)
        if n > 0:
            given = (new_k, new_v)[n - 1]
            for q in range(2):
                given[q] = buffer[pl.ds(q * GROUP, GROUP), :]

    nt = (((1,), (1,)), ((), ()))

    def attend(q):
        need("k", "v")
        rows = pl.ds(q * GROUP, GROUP)
        query = qbuf[rows, :]
        old = lax.dot_general(query, kcv[q], nt, preferred_element_type=F32) * (HD ** -0.5)
        fresh = lax.dot_general(query, kbuf[rows, :], nt, preferred_element_type=F32) * (HD ** -0.5)
        place = lax.broadcasted_iota(jnp.int32, (GROUP, SLOTS), 1)
        old = jnp.where(place < lens[q], old, very_low)
        i0 = lax.broadcasted_iota(jnp.int32, (GROUP, GROUP), 0)
        i1 = lax.broadcasted_iota(jnp.int32, (GROUP, GROUP), 1)
        fresh = jnp.where(i1 <= i0, fresh, very_low)
        top = jnp.maximum(jnp.max(old, axis=1, keepdims=True), jnp.max(fresh, axis=1, keepdims=True))
        old = jnp.exp(old - top)
        fresh = jnp.exp(fresh - top)
        total = jnp.sum(old, axis=1, keepdims=True) + jnp.sum(fresh, axis=1, keepdims=True)
        mixed = jnp.dot(old.astype(BF16), vcv[q], preferred_element_type=F32)
        mixed += jnp.dot(fresh.astype(BF16), vbuf[rows, :], preferred_element_type=F32)
        ctx[rows, :] = (mixed / total).astype(BF16)


    def feed(n):
        need("u")
        cols = slice(n * 256, n * 256 + 256)
        upward = jnp.dot(nrm[...], wub[:, cols], preferred_element_type=F32) + ubv[:, cols]
        act[:, cols] = jax.nn.gelu(upward, approximate=True).astype(BF16)

    def block(g, t):
        o = 4 * t + g
        weight = jnp.concatenate([wdb[o], wdb[o + 2]], axis=1)
        cols = [pl.ds(pl.multiple_of((o + 2 * i) * 128, 128), 128) for i in range(2)]
        last = jnp.concatenate([wov[:, cols[0]], wov[:, cols[1]]], axis=1)
        part[g, t] = jnp.dot(act[...], weight, preferred_element_type=F32) + jnp.dot(
            ctx[...], last, preferred_element_type=F32
        )

    def hop(g, direction, s, c):
        k = ((g * 2 + direction) * 4 + s) * 4 + c
        rows = pl.ds(64 * c, 64)
        return remote(
            rsend.at[g, direction, s, rows, :], rrecv.at[g, direction, s, rows, :],
            ss.at[k], sr.at[k], (r, z_plus if direction == 0 else z_minus),
        )

    def pieces(direction, s):
        return range(4) if s > 0 else range(2 * direction, 2 * direction + 2)

    def hand_on(g, s):
        for c in (0, 1, 2, 3):
            rows = pl.ds(64 * c, 64)
            for direction in range(2):
                if c not in pieces(direction, s):
                    continue
                t = (z + 4 - s) % Z if direction == 0 else (z + 4 + s) % Z
                value = part[g, t, rows, :]
                if s > 0 and c in pieces(direction, s - 1):
                    hop(g, direction, s - 1, c).wait_recv()
                    value += rrecv[g, direction, s - 1, rows, :].astype(F32)
                rsend[g, direction, s, rows, :] = value.astype(BF16)
                copy = hop(g, direction, s, c)
                copy.start()
                sent.append(copy)

    def finish(g):
        for c in range(4):
            rows = pl.ds(64 * c, 64)
            total = part[g, z, rows, :]
            for direction in range(2):
                hop(g, direction, 3, c).wait_recv()
                total += rrecv[g, direction, 3, rows, :].astype(F32)
            for i in range(2):
                cols = slice(256 * i + 128 * g, 256 * i + 128 * g + 128)
                mine = xg[z, rows, cols].astype(F32)
                out[rows, cols] = (mine + total[:, 128 * i:128 * (i + 1)] + dbv[:, cols]).astype(BF16)

    def blocks(g, s):
        need("o")
        if s in (0, 4):
            block(g, (z + 4 - s) % Z)
        else:
            block(g, (z + 4 - s) % Z)
            block(g, (z + 4 + s) % Z)

    def both(distance, c):
        for direction in range(2):
            if distance <= zlast(direction, c):
                zevent(direction, distance, c)

    steps = {
        "Z": both, "F": first_event, "H": first_halves, "S": second_event, "T": second_halves,
        "P": partner_waits, "B": blocks, "N": hand_on, "E": finish, "own": start_own,
        "ln": norm, "project": project, "at": attend, "up": feed,
    }
    for step in ORDER:
        steps[step[0]](*step[1:])
    for copy in sent:
        copy.wait_send()


def body(
    hidden_in, norm_gain, norm_shift, attend_weight, output_weight, up_weight,
    up_bias, down_weight, down_bias, key_cache, value_cache, cached_len,
):
    lanes = np.arange(128)
    freq = np.where(lanes < ROT, 10000.0 ** (-(2.0 * (lanes // 2)) / ROT), 0.0)
    steps = np.arange(GROUP)[:, None] * freq[None, :]
    tables = np.concatenate([np.tile(freq, (8, 1)), np.cos(steps), np.sin(steps)], axis=0)
    freq = jnp.asarray(tables, dtype=F32)
    anywhere = pl.BlockSpec(memory_space=pltpu.HBM)
    vmem = pl.BlockSpec(memory_space=pltpu.VMEM)
    dma = pltpu.SemaphoreType.DMA
    return pl.pallas_call(
        kernel,
        out_shape=(
            jax.ShapeDtypeStruct((TOK, COLS), BF16),
            jax.ShapeDtypeStruct((2, GROUP, HD), BF16),
            jax.ShapeDtypeStruct((2, GROUP, HD), BF16),
        ),
        in_specs=[anywhere] * 13,
        out_specs=(vmem, vmem, vmem),
        scratch_shapes=[
            pltpu.VMEM((Z, TOK, COLS), BF16),
            pltpu.VMEM((TOK, D), BF16),
            pltpu.VMEM((D, UNITS), BF16),
            pltpu.VMEM((32, UNITS, 128), BF16),
            pltpu.VMEM((3, D, HD), BF16),
            pltpu.VMEM((HD, D), BF16),
            pltpu.VMEM((2, SLOTS, HD), BF16),
            pltpu.VMEM((2, SLOTS, HD), BF16),
            pltpu.VMEM((1, D), F32),
            pltpu.VMEM((1, D), F32),
            pltpu.VMEM((1, UNITS), F32),
            pltpu.VMEM((1, COLS), F32),
            pltpu.VMEM((8 + 2 * GROUP, 128), F32),
            pltpu.VMEM((TOK, HD), BF16),
            pltpu.VMEM((TOK, HD), BF16),
            pltpu.VMEM((TOK, HD), BF16),
            pltpu.VMEM((TOK, HD), BF16),
            pltpu.VMEM((TOK, UNITS), BF16),
            pltpu.VMEM((2, Z, TOK, 256), F32),
            pltpu.VMEM((2, 2, 4, TOK, 256), BF16),
            pltpu.VMEM((2, 2, 4, TOK, 256), BF16),
            pltpu.SMEM((2,), jnp.int32),
            dma((13,)),
            dma((16,)),
            dma((16,)),
            dma((3, 36)),
            dma((3, 36)),
            dma((64,)),
            dma((64,)),
            dma((1,)),
            dma((1,)),
        ],
        compiler_params=pltpu.CompilerParams(
            collective_id=0, has_side_effects=True, vmem_limit_bytes=50 * 1000 * 1000
        ),
    )(
        *[
            pltpu.with_memory_space_constraint(v, pltpu.HBM)
            for v in (
                hidden_in, norm_gain[None, :], norm_shift[None, :],
                jnp.transpose(attend_weight, (1, 0, 2)), output_weight, up_weight,
                up_bias[None, :], down_weight, down_bias[None, :], key_cache, value_cache, freq,
                cached_len,
            )
        ]
    )


def solution(mesh):
    placed = (
        P("req", "head"), P(), P(), P(None, None, "head"), P("head", None), P("req", "head"),
        P("head"), P("head", "req"), P("head"), P("req", None, "head"), P("req", None, "head"), P("req"),
    )
    return jax.shard_map(
        body,
        mesh=mesh,
        in_specs=placed,
        out_specs=(P("req", "head"), P("req", None, "head"), P("req", None, "head")),
        check_vma=False,
    )
```

```python
import functools

import jax
import jax.numpy as jnp
import numpy as np
from jax import lax
from jax.experimental import pallas as pl
from jax.experimental.pallas import tpu as pltpu
from jax.sharding import PartitionSpec as P

HD = 256
ROT = 64
GROUP = 128
D = 4096
TOK = 256
UNITS = 1024
SLOTS = 1536
Z = 8
COLS = D // Z
epsilon = 1e-05
very_low = -1e30
ORDER = (
    ("Z", 1, 0), ("F", 0), ("S", 0, 0), ("Z", 1, 1), ("F", 1), ("Z", 2, 0), ("H", 0), ("Z", 2, 1),
    ("S", 0, 1), ("H", 1), ("S", 0, 2), ("Z", 3, 0), ("Z", 3, 1), ("S", 1, 2), ("T", 0, 0), ("S", 1, 1),
    ("Z", 4, 1), ("Z", 4, 0), ("ln", 0), ("S", 0, 3), ("S", 1, 0), ("ln", 1), ("T", 0, 1), ("project", 2),
    ("S", 1, 3), ("project", 1), ("project", 0), ("T", 1, 2), ("T", 0, 2), ("at", 1), ("T", 1, 1), ("own", 2),
    ("T", 1, 0), ("T", 0, 3), ("at", 0), ("T", 1, 3), ("P", 0), ("up", 3), ("up", 0), ("S", 2, 0),
    ("F", 2), ("up", 2), ("up", 1), ("P", 1), ("B", 0, 0), ("N", 0, 0), ("T", 2, 0), ("H", 2),
    ("B", 0, 2), ("B", 0, 1), ("S", 2, 1), ("N", 0, 1), ("S", 2, 2), ("S", 2, 3), ("T", 2, 1), ("B", 0, 3),
    ("T", 2, 2), ("N", 0, 2), ("T", 2, 3), ("P", 2), ("B", 1, 0), ("N", 1, 0), ("N", 0, 3), ("B", 1, 1),
    ("N", 1, 1), ("B", 1, 2), ("B", 0, 4), ("B", 1, 4), ("E", 0), ("N", 1, 2), ("B", 1, 3), ("N", 1, 3),
    ("E", 1),
)
MESH = pl.DeviceIdType.MESH
F32 = jnp.float32
BF16 = jnp.bfloat16


def kernel(
    hid, gain, shift, wq, wo, wu, ub, wd, db, kc, vc, freq, lens_in,
    out, new_k, new_v,
    xg, nrm, wub, wdb, wqv, wov, kcv, vcv, gainv, shiftv, ubv, dbv, freqv,
    qbuf, kbuf, vbuf, ctx, act, part, rsend, rrecv, lens,
    local_sem, zs, zr, ws, wr, ss, sr, xs, xr,
):
    r = lax.axis_index("req")
    z = lax.axis_index("head")
    core = r % 2
    y = (r // 2) % 4
    x = r // 8

    def device(c, a_, b_):
        x_ = (1 - c) * a_ + c * b_
        y_ = (1 - c) * b_ + c * a_
        return ((x_ % 4) * 4 + (y_ % 4)) * 2 + c

    a = (1 - core) * x + core * y
    b = (1 - core) * y + core * x
    partner = device(1 - core, b, a)
    a_plus, a_minus = device(core, a + 1, b), device(core, a + 3, b)
    b_plus, b_minus = device(core, a, b + 1), device(core, a, b + 3)
    z_plus, z_minus = (z + 1) % Z, (z + 7) % Z

    barrier = pltpu.get_barrier_semaphore()
    for who in (
        (a_plus, z), (a_minus, z), (b_plus, z), (b_minus, z), (partner, z),
        (r, z_plus), (r, z_minus),
    ):
        pl.semaphore_signal(barrier, inc=1, device_id=who, device_id_type=MESH)
    pl.semaphore_wait(barrier, 7)

    sent = []

    def remote(src, dst, send, recv, who):
        return pltpu.make_async_remote_copy(
            src_ref=src, dst_ref=dst, send_sem=send, recv_sem=recv,
            device_id=who, device_id_type=MESH,
        )

    def launch(src, dst, send, recv, who):
        copy = remote(src, dst, send, recv, who)
        copy.start()
        sent.append(copy)

    def zchunk(origin, c):
        return xg.at[origin, pl.ds(128 * c, 128), :]

    def zindex(direction, hop, c):
        return direction * 8 + (hop - 1) * 2 + c

    def zsend(direction, hop, c):
        origin = (z + Z - (hop - 1)) % Z if direction == 0 else (z + hop - 1) % Z
        src = hid.at[pl.ds(128 * c, 128), :] if hop == 1 else zchunk(origin, c)
        k = zindex(direction, hop, c)
        launch(src, zchunk(origin, c), zs.at[k], zr.at[k], (r, z_plus if direction == 0 else z_minus))

    def zwait(direction, hop, c):
        origin = (z + Z - hop) % Z if direction == 0 else (z + hop) % Z
        k = zindex(direction, hop, c)
        view = zchunk(origin, c)
        remote(view, view, zs.at[k], zr.at[k], (r, z_plus)).wait_recv()

    def zlast(direction, c):
        return 4 if c == direction else 3

    def zevent(direction, hop, c):
        zwait(direction, hop, c)
        if hop < zlast(direction, c):
            zsend(direction, hop + 1, c)

    def slot(w, o):
        if w == 0:
            return wub.at[pl.ds(pl.multiple_of(o * 128, 128), 128), :]
        return wdb.at[(o // 2) * 2 + w - 1, pl.ds(pl.multiple_of((o % 2) * 512, 512), 512), :]

    def half(w, o, k):
        if w == 0:
            return wub.at[pl.ds(pl.multiple_of(o * 128 + 64 * k, 64), 64), :]
        return wdb.at[(o // 2) * 2 + w - 1, pl.ds(pl.multiple_of((o % 2) * 512 + 256 * k, 256), 256), :]

    A_OF = (0, 3, 1, 2)

    def wsend(w, k, src, dst, who):
        launch(src, dst, ws.at[w, k], wr.at[w, k], (who, z))

    def wwait(w, k, view):
        remote(view, view, ws.at[w, k], wr.at[w, k], (partner, z)).wait_recv()

    def across(w, j, kb):
        o = device(core, a + A_OF[j], b + A_OF[kb])
        src = wu if w == 0 and j == 0 and kb == 0 else slot(w, o)
        wsend(w, 20 + 4 * j + kb, src, slot(w, o), partner)

    def second(w, j):
        o = device(core, a + A_OF[j], b)
        src = wu if w == 0 and j == 0 else slot(w, o)
        wsend(w, 4 + 4 * j, src, slot(w, o), b_plus)
        wsend(w, 5 + 4 * j, src, slot(w, o), b_minus)

    def start_own(w):
        src = wu if w == 0 else slot(w, r)
        wsend(w, 0, src, slot(w, r), a_plus)
        wsend(w, 1, src, slot(w, r), a_minus)
        second(w, 0)
        if w == 0:
            across(w, 0, 0)

    def first_event(w):
        o = device(core, a + 3, b)
        wwait(w, 0, slot(w, o))
        wsend(w, 2, half(w, o, 0), half(w, o, 0), a_plus)
        o = device(core, a + 1, b)
        wwait(w, 1, slot(w, o))
        wsend(w, 3, half(w, o, 1), half(w, o, 1), a_minus)
        second(w, 1)
        second(w, 2)
        across(w, 1, 0)
        across(w, 2, 0)

    def first_halves(w):
        o = device(core, a + 2, b)
        wwait(w, 2, half(w, o, 0))
        wwait(w, 3, half(w, o, 1))
        second(w, 3)
        across(w, 3, 0)

    def second_event(w, j):
        aj = a + A_OF[j]
        o = device(core, aj, b + 3)
        wwait(w, 4 + 4 * j, slot(w, o))
        wsend(w, 6 + 4 * j, half(w, o, 0), half(w, o, 0), b_plus)
        o = device(core, aj, b + 1)
        wwait(w, 5 + 4 * j, slot(w, o))
        wsend(w, 7 + 4 * j, half(w, o, 1), half(w, o, 1), b_minus)
        across(w, j, 1)
        across(w, j, 2)

    def second_halves(w, j):
        o = device(core, a + A_OF[j], b + 2)
        wwait(w, 6 + 4 * j, half(w, o, 0))
        wwait(w, 7 + 4 * j, half(w, o, 1))
        across(w, j, 3)

    def partner_waits(w):
        for j in range(4):
            for kb in range(4):
                if w > 0 and j == 0 and kb == 0:
                    continue
                o = device(1 - core, b + A_OF[j], a + A_OF[kb])
                wwait(w, 20 + 4 * j + kb, slot(w, o))

    locals_ = []
    pending = {}

    def need(*names):
        for name in names:
            if name in pending:
                pending.pop(name).wait()

    def bring(src, dst):
        copy = pltpu.make_async_copy(src, dst, local_sem.at[len(locals_)])
        copy.start()
        locals_.append(copy)
        return copy

    for c in range(2):
        zsend(0, 1, c)
        zsend(1, 1, c)
    start_own(0)
    launch(wd, wdb.at[r], xs.at[0], xr.at[0], (partner, z))
    c_d = bring(wd, wdb.at[r])
    pending["x"] = bring(hid, xg.at[z])
    c_small = [bring(lens_in, lens), bring(gain, gainv), bring(shift, shiftv), bring(ub, ubv), bring(db, dbv), bring(freq, freqv)]
    pending["u"] = bring(wu, slot(0, r))
    pending["q"] = bring(wq, wqv)
    pending["k"] = bring(kc, kcv)
    pending["v"] = bring(vc, vcv)
    pending["o"] = bring(wo, wov)
    for copy in c_small:
        copy.wait()
    c_d.wait()
    remote(wdb.at[partner], wdb.at[partner], xs.at[0], xr.at[0], (partner, z)).wait_recv()
    start_own(1)

    lane = lax.broadcasted_iota(jnp.int32, (TOK, 128), 1)
    turn = [lens[q].astype(F32) * freqv[pl.ds(0, 8), :] for q in range(2)]

    def rotation():
        cosines, sines = [], []
        for q in range(2):
            cl, sl = jnp.cos(turn[q])[:1], jnp.sin(turn[q])[:1]
            ct, st = freqv[pl.ds(8, GROUP), :], freqv[pl.ds(8 + GROUP, GROUP), :]
            cosines.append(cl * ct - sl * st)
            sines.append(sl * ct + cl * st)
        cosine = jnp.concatenate(cosines, axis=0)
        sine = jnp.concatenate(sines, axis=0)
        return cosine, jnp.where(lane % 2 == 0, -sine, sine)

    def rotate(t, cosine, sine):
        head = t[:, :128]
        swapped = jnp.where(lane % 2 == 0, pltpu.roll(head, 127, 1), pltpu.roll(head, 1, 1))
        return jnp.concatenate([head * cosine + swapped * sine, t[:, 128:]], axis=1)

    def norm(n):
        need("x")

        @pl.loop(n * 8, n * 8 + 8)
        def _(i):
            rows = pl.ds(pl.multiple_of(i * 16, 16), 16)
            total = jnp.zeros((16, 1), F32)
            for h in range(Z):
                total += jnp.sum(xg[h, rows, :].astype(F32), axis=1, keepdims=True)
            mean = total * (1.0 / D)
            square = jnp.zeros((16, 1), F32)
            for h in range(Z):
                center = xg[h, rows, :].astype(F32) - mean
                square += jnp.sum(center * center, axis=1, keepdims=True)
            scale = lax.rsqrt(square * (1.0 / D) + epsilon)
            for h in range(Z):
                cols = slice(h * COLS, (h + 1) * COLS)
                center = xg[h, rows, :].astype(F32) - mean
                nrm[rows, cols] = (center * scale * gainv[:, cols] + shiftv[:, cols]).astype(BF16)

    def project(n):
        need("q")
        value = jnp.dot(nrm[...], wqv[n], preferred_element_type=F32)
        if n < 2:
            value = rotate(value, *rotation())
        buffer = (qbuf, kbuf, vbuf)[n]
        buffer[...] = value.astype(BF16)
        if n > 0:
            given = (new_k, new_v)[n - 1]
            for q in range(2):
                given[q] = buffer[pl.ds(q * GROUP, GROUP), :]

    nt = (((1,), (1,)), ((), ()))

    def attend(q):
        need("k", "v")
        rows = pl.ds(q * GROUP, GROUP)
        query = qbuf[rows, :]
        old = lax.dot_general(query, kcv[q], nt, preferred_element_type=F32) * (HD ** -0.5)
        fresh = lax.dot_general(query, kbuf[rows, :], nt, preferred_element_type=F32) * (HD ** -0.5)
        place = lax.broadcasted_iota(jnp.int32, (GROUP, SLOTS), 1)
        old = jnp.where(place < lens[q], old, very_low)
        i0 = lax.broadcasted_iota(jnp.int32, (GROUP, GROUP), 0)
        i1 = lax.broadcasted_iota(jnp.int32, (GROUP, GROUP), 1)
        fresh = jnp.where(i1 <= i0, fresh, very_low)
        top = jnp.maximum(jnp.max(old, axis=1, keepdims=True), jnp.max(fresh, axis=1, keepdims=True))
        old = jnp.exp(old - top)
        fresh = jnp.exp(fresh - top)
        total = jnp.sum(old, axis=1, keepdims=True) + jnp.sum(fresh, axis=1, keepdims=True)
        mixed = jnp.dot(old.astype(BF16), vcv[q], preferred_element_type=F32)
        mixed += jnp.dot(fresh.astype(BF16), vbuf[rows, :], preferred_element_type=F32)
        ctx[rows, :] = (mixed / total).astype(BF16)


    def feed(n):
        need("u")
        cols = slice(n * 256, n * 256 + 256)
        upward = jnp.dot(nrm[...], wub[:, cols], preferred_element_type=F32) + ubv[:, cols]
        act[:, cols] = jax.nn.gelu(upward, approximate=True).astype(BF16)

    def block(g, t):
        o = 4 * t + g
        weight = jnp.concatenate([wdb[o], wdb[o + 2]], axis=1)
        cols = [pl.ds(pl.multiple_of((o + 2 * i) * 128, 128), 128) for i in range(2)]
        last = jnp.concatenate([wov[:, cols[0]], wov[:, cols[1]]], axis=1)
        part[g, t] = jnp.dot(act[...], weight, preferred_element_type=F32) + jnp.dot(
            ctx[...], last, preferred_element_type=F32
        )

    def hop(g, direction, s, c):
        k = ((g * 2 + direction) * 4 + s) * 4 + c
        rows = pl.ds(64 * c, 64)
        return remote(
            rsend.at[g, direction, s, rows, :], rrecv.at[g, direction, s, rows, :],
            ss.at[k], sr.at[k], (r, z_plus if direction == 0 else z_minus),
        )

    def pieces(direction, s):
        return range(4) if s > 0 else range(2 * direction, 2 * direction + 2)

    def hand_on(g, s):
        for c in (0, 1, 2, 3):
            rows = pl.ds(64 * c, 64)
            for direction in range(2):
                if c not in pieces(direction, s):
                    continue
                t = (z + 4 - s) % Z if direction == 0 else (z + 4 + s) % Z
                value = part[g, t, rows, :]
                if s > 0 and c in pieces(direction, s - 1):
                    hop(g, direction, s - 1, c).wait_recv()
                    value += rrecv[g, direction, s - 1, rows, :].astype(F32)
                rsend[g, direction, s, rows, :] = value.astype(BF16)
                copy = hop(g, direction, s, c)
                copy.start()
                sent.append(copy)

    def finish(g):
        for c in range(4):
            rows = pl.ds(64 * c, 64)
            total = part[g, z, rows, :]
            for direction in range(2):
                hop(g, direction, 3, c).wait_recv()
                total += rrecv[g, direction, 3, rows, :].astype(F32)
            for i in range(2):
                cols = slice(256 * i + 128 * g, 256 * i + 128 * g + 128)
                mine = xg[z, rows, cols].astype(F32)
                out[rows, cols] = (mine + total[:, 128 * i:128 * (i + 1)] + dbv[:, cols]).astype(BF16)

    def blocks(g, s):
        need("o")
        if s in (0, 4):
            block(g, (z + 4 - s) % Z)
        else:
            block(g, (z + 4 - s) % Z)
            block(g, (z + 4 + s) % Z)

    def both(distance, c):
        for direction in range(2):
            if distance <= zlast(direction, c):
                zevent(direction, distance, c)

    steps = {
        "Z": both, "F": first_event, "H": first_halves, "S": second_event, "T": second_halves,
        "P": partner_waits, "B": blocks, "N": hand_on, "E": finish, "own": start_own,
        "ln": norm, "project": project, "at": attend, "up": feed,
    }
    for step in ORDER:
        steps[step[0]](*step[1:])
    for copy in sent:
        copy.wait_send()


def body(
    hidden_in, norm_gain, norm_shift, attend_weight, output_weight, up_weight,
    up_bias, down_weight, down_bias, key_cache, value_cache, cached_len,
):
    lanes = np.arange(128)
    freq = np.where(lanes < ROT, 10000.0 ** (-(2.0 * (lanes // 2)) / ROT), 0.0)
    steps = np.arange(GROUP)[:, None] * freq[None, :]
    tables = np.concatenate([np.tile(freq, (8, 1)), np.cos(steps), np.sin(steps)], axis=0)
    freq = jnp.asarray(tables, dtype=F32)
    anywhere = pl.BlockSpec(memory_space=pltpu.HBM)
    vmem = pl.BlockSpec(memory_space=pltpu.VMEM)
    dma = pltpu.SemaphoreType.DMA
    return pl.pallas_call(
        kernel,
        out_shape=(
            jax.ShapeDtypeStruct((TOK, COLS), BF16),
            jax.ShapeDtypeStruct((2, GROUP, HD), BF16),
            jax.ShapeDtypeStruct((2, GROUP, HD), BF16),
        ),
        in_specs=[anywhere] * 13,
        out_specs=(vmem, vmem, vmem),
        scratch_shapes=[
            pltpu.VMEM((Z, TOK, COLS), BF16),
            pltpu.VMEM((TOK, D), BF16),
            pltpu.VMEM((D, UNITS), BF16),
            pltpu.VMEM((32, UNITS, 128), BF16),
            pltpu.VMEM((3, D, HD), BF16),
            pltpu.VMEM((HD, D), BF16),
            pltpu.VMEM((2, SLOTS, HD), BF16),
            pltpu.VMEM((2, SLOTS, HD), BF16),
            pltpu.VMEM((1, D), F32),
            pltpu.VMEM((1, D), F32),
            pltpu.VMEM((1, UNITS), F32),
            pltpu.VMEM((1, COLS), F32),
            pltpu.VMEM((8 + 2 * GROUP, 128), F32),
            pltpu.VMEM((TOK, HD), BF16),
            pltpu.VMEM((TOK, HD), BF16),
            pltpu.VMEM((TOK, HD), BF16),
            pltpu.VMEM((TOK, HD), BF16),
            pltpu.VMEM((TOK, UNITS), BF16),
            pltpu.VMEM((2, Z, TOK, 256), F32),
            pltpu.VMEM((2, 2, 4, TOK, 256), BF16),
            pltpu.VMEM((2, 2, 4, TOK, 256), BF16),
            pltpu.SMEM((2,), jnp.int32),
            dma((13,)),
            dma((16,)),
            dma((16,)),
            dma((3, 36)),
            dma((3, 36)),
            dma((64,)),
            dma((64,)),
            dma((1,)),
            dma((1,)),
        ],
        compiler_params=pltpu.CompilerParams(
            collective_id=0, has_side_effects=True, vmem_limit_bytes=50 * 1000 * 1000
        ),
    )(
        *[
            pltpu.with_memory_space_constraint(v, pltpu.HBM)
            for v in (
                hidden_in, norm_gain[None, :], norm_shift[None, :],
                jnp.transpose(attend_weight, (1, 0, 2)), output_weight, up_weight,
                up_bias[None, :], down_weight, down_bias[None, :], key_cache, value_cache, freq,
                cached_len,
            )
        ]
    )


def solution(mesh):
    placed = (
        P("req", "head"), P(), P(), P(None, None, "head"), P("head", None), P("req", "head"),
        P("head"), P("head", "req"), P("head"), P("req", None, "head"), P("req", None, "head"), P("req"),
    )
    return jax.shard_map(
        body,
        mesh=mesh,
        in_specs=placed,
        out_specs=(P("req", "head"), P("req", None, "head"), P("req", None, "head")),
        check_vma=False,
    )
```

```python
import functools

import jax
import jax.numpy as jnp
import numpy as np
from jax import lax
from jax.experimental import pallas as pl
from jax.experimental.pallas import tpu as pltpu
from jax.sharding import PartitionSpec as P

HD = 256
ROT = 64
GROUP = 128
D = 4096
TOK = 256
UNITS = 1024
SLOTS = 1536
Z = 8
COLS = D // Z
epsilon = 1e-05
very_low = -1e30
ORDER = (
    ("Z", 1, 0), ("F", 0), ("S", 0, 0), ("Z", 1, 1), ("F", 1), ("Z", 2, 0), ("H", 0), ("Z", 2, 1),
    ("S", 0, 1), ("H", 1), ("S", 0, 2), ("Z", 3, 0), ("Z", 3, 1), ("S", 1, 2), ("T", 0, 0), ("S", 1, 1),
    ("Z", 4, 1), ("Z", 4, 0), ("ln", 0), ("S", 0, 3), ("S", 1, 0), ("ln", 1), ("T", 0, 1), ("project", 2),
    ("S", 1, 3), ("own", 2), ("project", 1), ("project", 0), ("T", 1, 2), ("T", 0, 2), ("at", 1), ("T", 1, 1),
    ("T", 1, 0), ("T", 0, 3), ("at", 0), ("T", 1, 3), ("P", 0), ("up", 3), ("up", 0), ("S", 2, 0),
    ("F", 2), ("up", 2), ("up", 1), ("P", 1), ("B", 0, 0), ("N", 0, 0), ("T", 2, 0), ("H", 2),
    ("B", 0, 2), ("B", 0, 1), ("S", 2, 1), ("N", 0, 1), ("S", 2, 2), ("S", 2, 3), ("T", 2, 1), ("B", 0, 3),
    ("T", 2, 2), ("N", 0, 2), ("T", 2, 3), ("P", 2), ("B", 1, 0), ("N", 1, 0), ("N", 0, 3), ("B", 1, 1),
    ("N", 1, 1), ("B", 1, 2), ("B", 0, 4), ("B", 1, 4), ("E", 0), ("N", 1, 2), ("B", 1, 3), ("N", 1, 3),
    ("E", 1),
)
MESH = pl.DeviceIdType.MESH
F32 = jnp.float32
BF16 = jnp.bfloat16


def kernel(
    hid, gain, shift, wq, wo, wu, ub, wd, db, kc, vc, freq, lens_in,
    out, new_k, new_v,
    xg, nrm, wub, wdb, wqv, wov, kcv, vcv, gainv, shiftv, ubv, dbv, freqv,
    qbuf, kbuf, vbuf, ctx, act, part, rsend, rrecv, lens,
    local_sem, zs, zr, ws, wr, ss, sr, xs, xr,
):
    r = lax.axis_index("req")
    z = lax.axis_index("head")
    core = r % 2
    y = (r // 2) % 4
    x = r // 8

    def device(c, a_, b_):
        x_ = (1 - c) * a_ + c * b_
        y_ = (1 - c) * b_ + c * a_
        return ((x_ % 4) * 4 + (y_ % 4)) * 2 + c

    a = (1 - core) * x + core * y
    b = (1 - core) * y + core * x
    partner = device(1 - core, b, a)
    a_plus, a_minus = device(core, a + 1, b), device(core, a + 3, b)
    b_plus, b_minus = device(core, a, b + 1), device(core, a, b + 3)
    z_plus, z_minus = (z + 1) % Z, (z + 7) % Z

    barrier = pltpu.get_barrier_semaphore()
    for who in (
        (a_plus, z), (a_minus, z), (b_plus, z), (b_minus, z), (partner, z),
        (r, z_plus), (r, z_minus),
    ):
        pl.semaphore_signal(barrier, inc=1, device_id=who, device_id_type=MESH)
    pl.semaphore_wait(barrier, 7)

    sent = []

    def remote(src, dst, send, recv, who):
        return pltpu.make_async_remote_copy(
            src_ref=src, dst_ref=dst, send_sem=send, recv_sem=recv,
            device_id=who, device_id_type=MESH,
        )

    def launch(src, dst, send, recv, who):
        copy = remote(src, dst, send, recv, who)
        copy.start()
        sent.append(copy)

    def zchunk(origin, c):
        return xg.at[origin, pl.ds(128 * c, 128), :]

    def zindex(direction, hop, c):
        return direction * 8 + (hop - 1) * 2 + c

    def zsend(direction, hop, c):
        origin = (z + Z - (hop - 1)) % Z if direction == 0 else (z + hop - 1) % Z
        src = hid.at[pl.ds(128 * c, 128), :] if hop == 1 else zchunk(origin, c)
        k = zindex(direction, hop, c)
        launch(src, zchunk(origin, c), zs.at[k], zr.at[k], (r, z_plus if direction == 0 else z_minus))

    def zwait(direction, hop, c):
        origin = (z + Z - hop) % Z if direction == 0 else (z + hop) % Z
        k = zindex(direction, hop, c)
        view = zchunk(origin, c)
        remote(view, view, zs.at[k], zr.at[k], (r, z_plus)).wait_recv()

    def zlast(direction, c):
        return 4 if c == direction else 3

    def zevent(direction, hop, c):
        zwait(direction, hop, c)
        if hop < zlast(direction, c):
            zsend(direction, hop + 1, c)

    def slot(w, o):
        if w == 0:
            return wub.at[pl.ds(pl.multiple_of(o * 128, 128), 128), :]
        return wdb.at[(o // 2) * 2 + w - 1, pl.ds(pl.multiple_of((o % 2) * 512, 512), 512), :]

    def half(w, o, k):
        if w == 0:
            return wub.at[pl.ds(pl.multiple_of(o * 128 + 64 * k, 64), 64), :]
        return wdb.at[(o // 2) * 2 + w - 1, pl.ds(pl.multiple_of((o % 2) * 512 + 256 * k, 256), 256), :]

    A_OF = (0, 3, 1, 2)

    def wsend(w, k, src, dst, who):
        launch(src, dst, ws.at[w, k], wr.at[w, k], (who, z))

    def wwait(w, k, view):
        remote(view, view, ws.at[w, k], wr.at[w, k], (partner, z)).wait_recv()

    def across(w, j, kb):
        o = device(core, a + A_OF[j], b + A_OF[kb])
        src = wu if w == 0 and j == 0 and kb == 0 else slot(w, o)
        wsend(w, 20 + 4 * j + kb, src, slot(w, o), partner)

    def second(w, j):
        o = device(core, a + A_OF[j], b)
        src = wu if w == 0 and j == 0 else slot(w, o)
        wsend(w, 4 + 4 * j, src, slot(w, o), b_plus)
        wsend(w, 5 + 4 * j, src, slot(w, o), b_minus)

    def start_own(w):
        src = wu if w == 0 else slot(w, r)
        wsend(w, 0, src, slot(w, r), a_plus)
        wsend(w, 1, src, slot(w, r), a_minus)
        second(w, 0)
        if w == 0:
            across(w, 0, 0)

    def first_event(w):
        o = device(core, a + 3, b)
        wwait(w, 0, slot(w, o))
        wsend(w, 2, half(w, o, 0), half(w, o, 0), a_plus)
        o = device(core, a + 1, b)
        wwait(w, 1, slot(w, o))
        wsend(w, 3, half(w, o, 1), half(w, o, 1), a_minus)
        second(w, 1)
        second(w, 2)
        across(w, 1, 0)
        across(w, 2, 0)

    def first_halves(w):
        o = device(core, a + 2, b)
        wwait(w, 2, half(w, o, 0))
        wwait(w, 3, half(w, o, 1))
        second(w, 3)
        across(w, 3, 0)

    def second_event(w, j):
        aj = a + A_OF[j]
        o = device(core, aj, b + 3)
        wwait(w, 4 + 4 * j, slot(w, o))
        wsend(w, 6 + 4 * j, half(w, o, 0), half(w, o, 0), b_plus)
        o = device(core, aj, b + 1)
        wwait(w, 5 + 4 * j, slot(w, o))
        wsend(w, 7 + 4 * j, half(w, o, 1), half(w, o, 1), b_minus)
        across(w, j, 1)
        across(w, j, 2)

    def second_halves(w, j):
        o = device(core, a + A_OF[j], b + 2)
        wwait(w, 6 + 4 * j, half(w, o, 0))
        wwait(w, 7 + 4 * j, half(w, o, 1))
        across(w, j, 3)

    def partner_waits(w):
        for j in range(4):
            for kb in range(4):
                if w > 0 and j == 0 and kb == 0:
                    continue
                o = device(1 - core, b + A_OF[j], a + A_OF[kb])
                wwait(w, 20 + 4 * j + kb, slot(w, o))

    locals_ = []
    pending = {}

    def need(*names):
        for name in names:
            if name in pending:
                pending.pop(name).wait()

    def bring(src, dst):
        copy = pltpu.make_async_copy(src, dst, local_sem.at[len(locals_)])
        copy.start()
        locals_.append(copy)
        return copy

    for c in range(2):
        zsend(0, 1, c)
        zsend(1, 1, c)
    start_own(0)
    launch(wd, wdb.at[r], xs.at[0], xr.at[0], (partner, z))
    c_d = bring(wd, wdb.at[r])
    pending["x"] = bring(hid, xg.at[z])
    c_small = [bring(lens_in, lens), bring(gain, gainv), bring(shift, shiftv), bring(ub, ubv), bring(db, dbv), bring(freq, freqv)]
    pending["u"] = bring(wu, slot(0, r))
    pending["q"] = bring(wq, wqv)
    pending["k"] = bring(kc, kcv)
    pending["v"] = bring(vc, vcv)
    pending["o"] = bring(wo, wov)
    for copy in c_small:
        copy.wait()
    c_d.wait()
    remote(wdb.at[partner], wdb.at[partner], xs.at[0], xr.at[0], (partner, z)).wait_recv()
    start_own(1)

    lane = lax.broadcasted_iota(jnp.int32, (TOK, 128), 1)
    turn = [lens[q].astype(F32) * freqv[pl.ds(0, 8), :] for q in range(2)]

    def rotation():
        cosines, sines = [], []
        for q in range(2):
            cl, sl = jnp.cos(turn[q])[:1], jnp.sin(turn[q])[:1]
            ct, st = freqv[pl.ds(8, GROUP), :], freqv[pl.ds(8 + GROUP, GROUP), :]
            cosines.append(cl * ct - sl * st)
            sines.append(sl * ct + cl * st)
        cosine = jnp.concatenate(cosines, axis=0)
        sine = jnp.concatenate(sines, axis=0)
        return cosine, jnp.where(lane % 2 == 0, -sine, sine)

    def rotate(t, cosine, sine):
        head = t[:, :128]
        swapped = jnp.where(lane % 2 == 0, pltpu.roll(head, 127, 1), pltpu.roll(head, 1, 1))
        return jnp.concatenate([head * cosine + swapped * sine, t[:, 128:]], axis=1)

    def norm(n):
        need("x")

        @pl.loop(n * 8, n * 8 + 8)
        def _(i):
            rows = pl.ds(pl.multiple_of(i * 16, 16), 16)
            total = jnp.zeros((16, 1), F32)
            for h in range(Z):
                total += jnp.sum(xg[h, rows, :].astype(F32), axis=1, keepdims=True)
            mean = total * (1.0 / D)
            square = jnp.zeros((16, 1), F32)
            for h in range(Z):
                center = xg[h, rows, :].astype(F32) - mean
                square += jnp.sum(center * center, axis=1, keepdims=True)
            scale = lax.rsqrt(square * (1.0 / D) + epsilon)
            for h in range(Z):
                cols = slice(h * COLS, (h + 1) * COLS)
                center = xg[h, rows, :].astype(F32) - mean
                nrm[rows, cols] = (center * scale * gainv[:, cols] + shiftv[:, cols]).astype(BF16)

    def project(n):
        need("q")
        value = jnp.dot(nrm[...], wqv[n], preferred_element_type=F32)
        if n < 2:
            value = rotate(value, *rotation())
        buffer = (qbuf, kbuf, vbuf)[n]
        buffer[...] = value.astype(BF16)
        if n > 0:
            given = (new_k, new_v)[n - 1]
            for q in range(2):
                given[q] = buffer[pl.ds(q * GROUP, GROUP), :]

    nt = (((1,), (1,)), ((), ()))

    def attend(q):
        need("k", "v")
        rows = pl.ds(q * GROUP, GROUP)
        query = qbuf[rows, :]
        old = lax.dot_general(query, kcv[q], nt, preferred_element_type=F32) * (HD ** -0.5)
        fresh = lax.dot_general(query, kbuf[rows, :], nt, preferred_element_type=F32) * (HD ** -0.5)
        place = lax.broadcasted_iota(jnp.int32, (GROUP, SLOTS), 1)
        old = jnp.where(place < lens[q], old, very_low)
        i0 = lax.broadcasted_iota(jnp.int32, (GROUP, GROUP), 0)
        i1 = lax.broadcasted_iota(jnp.int32, (GROUP, GROUP), 1)
        fresh = jnp.where(i1 <= i0, fresh, very_low)
        top = jnp.maximum(jnp.max(old, axis=1, keepdims=True), jnp.max(fresh, axis=1, keepdims=True))
        old = jnp.exp(old - top)
        fresh = jnp.exp(fresh - top)
        total = jnp.sum(old, axis=1, keepdims=True) + jnp.sum(fresh, axis=1, keepdims=True)
        mixed = jnp.dot(old.astype(BF16), vcv[q], preferred_element_type=F32)
        mixed += jnp.dot(fresh.astype(BF16), vbuf[rows, :], preferred_element_type=F32)
        ctx[rows, :] = (mixed / total).astype(BF16)


    def feed(n):
        need("u")
        cols = slice(n * 256, n * 256 + 256)
        upward = jnp.dot(nrm[...], wub[:, cols], preferred_element_type=F32) + ubv[:, cols]
        act[:, cols] = jax.nn.gelu(upward, approximate=True).astype(BF16)

    def block(g, t):
        o = 4 * t + g
        weight = jnp.concatenate([wdb[o], wdb[o + 2]], axis=1)
        cols = [pl.ds(pl.multiple_of((o + 2 * i) * 128, 128), 128) for i in range(2)]
        last = jnp.concatenate([wov[:, cols[0]], wov[:, cols[1]]], axis=1)
        part[g, t] = jnp.dot(act[...], weight, preferred_element_type=F32) + jnp.dot(
            ctx[...], last, preferred_element_type=F32
        )

    def hop(g, direction, s, c):
        k = ((g * 2 + direction) * 4 + s) * 4 + c
        rows = pl.ds(64 * c, 64)
        return remote(
            rsend.at[g, direction, s, rows, :], rrecv.at[g, direction, s, rows, :],
            ss.at[k], sr.at[k], (r, z_plus if direction == 0 else z_minus),
        )

    def pieces(direction, s):
        return range(4) if s > 0 else range(2 * direction, 2 * direction + 2)

    def hand_on(g, s):
        for c in (0, 1, 2, 3):
            rows = pl.ds(64 * c, 64)
            for direction in range(2):
                if c not in pieces(direction, s):
                    continue
                t = (z + 4 - s) % Z if direction == 0 else (z + 4 + s) % Z
                value = part[g, t, rows, :]
                if s > 0 and c in pieces(direction, s - 1):
                    hop(g, direction, s - 1, c).wait_recv()
                    value += rrecv[g, direction, s - 1, rows, :].astype(F32)
                rsend[g, direction, s, rows, :] = value.astype(BF16)
                copy = hop(g, direction, s, c)
                copy.start()
                sent.append(copy)

    def finish(g):
        for c in range(4):
            rows = pl.ds(64 * c, 64)
            total = part[g, z, rows, :]
            for direction in range(2):
                hop(g, direction, 3, c).wait_recv()
                total += rrecv[g, direction, 3, rows, :].astype(F32)
            for i in range(2):
                cols = slice(256 * i + 128 * g, 256 * i + 128 * g + 128)
                mine = xg[z, rows, cols].astype(F32)
                out[rows, cols] = (mine + total[:, 128 * i:128 * (i + 1)] + dbv[:, cols]).astype(BF16)

    def blocks(g, s):
        need("o")
        if s in (0, 4):
            block(g, (z + 4 - s) % Z)
        else:
            block(g, (z + 4 - s) % Z)
            block(g, (z + 4 + s) % Z)

    def both(distance, c):
        for direction in range(2):
            if distance <= zlast(direction, c):
                zevent(direction, distance, c)

    steps = {
        "Z": both, "F": first_event, "H": first_halves, "S": second_event, "T": second_halves,
        "P": partner_waits, "B": blocks, "N": hand_on, "E": finish, "own": start_own,
        "ln": norm, "project": project, "at": attend, "up": feed,
    }
    for step in ORDER:
        steps[step[0]](*step[1:])
    for copy in sent:
        copy.wait_send()


def body(
    hidden_in, norm_gain, norm_shift, attend_weight, output_weight, up_weight,
    up_bias, down_weight, down_bias, key_cache, value_cache, cached_len,
):
    lanes = np.arange(128)
    freq = np.where(lanes < ROT, 10000.0 ** (-(2.0 * (lanes // 2)) / ROT), 0.0)
    steps = np.arange(GROUP)[:, None] * freq[None, :]
    tables = np.concatenate([np.tile(freq, (8, 1)), np.cos(steps), np.sin(steps)], axis=0)
    freq = jnp.asarray(tables, dtype=F32)
    anywhere = pl.BlockSpec(memory_space=pltpu.HBM)
    vmem = pl.BlockSpec(memory_space=pltpu.VMEM)
    dma = pltpu.SemaphoreType.DMA
    return pl.pallas_call(
        kernel,
        out_shape=(
            jax.ShapeDtypeStruct((TOK, COLS), BF16),
            jax.ShapeDtypeStruct((2, GROUP, HD), BF16),
            jax.ShapeDtypeStruct((2, GROUP, HD), BF16),
        ),
        in_specs=[anywhere] * 13,
        out_specs=(vmem, vmem, vmem),
        scratch_shapes=[
            pltpu.VMEM((Z, TOK, COLS), BF16),
            pltpu.VMEM((TOK, D), BF16),
            pltpu.VMEM((D, UNITS), BF16),
            pltpu.VMEM((32, UNITS, 128), BF16),
            pltpu.VMEM((3, D, HD), BF16),
            pltpu.VMEM((HD, D), BF16),
            pltpu.VMEM((2, SLOTS, HD), BF16),
            pltpu.VMEM((2, SLOTS, HD), BF16),
            pltpu.VMEM((1, D), F32),
            pltpu.VMEM((1, D), F32),
            pltpu.VMEM((1, UNITS), F32),
            pltpu.VMEM((1, COLS), F32),
            pltpu.VMEM((8 + 2 * GROUP, 128), F32),
            pltpu.VMEM((TOK, HD), BF16),
            pltpu.VMEM((TOK, HD), BF16),
            pltpu.VMEM((TOK, HD), BF16),
            pltpu.VMEM((TOK, HD), BF16),
            pltpu.VMEM((TOK, UNITS), BF16),
            pltpu.VMEM((2, Z, TOK, 256), F32),
            pltpu.VMEM((2, 2, 4, TOK, 256), BF16),
            pltpu.VMEM((2, 2, 4, TOK, 256), BF16),
            pltpu.SMEM((2,), jnp.int32),
            dma((13,)),
            dma((16,)),
            dma((16,)),
            dma((3, 36)),
            dma((3, 36)),
            dma((64,)),
            dma((64,)),
            dma((1,)),
            dma((1,)),
        ],
        compiler_params=pltpu.CompilerParams(
            collective_id=0, has_side_effects=True, vmem_limit_bytes=50 * 1000 * 1000
        ),
    )(
        *[
            pltpu.with_memory_space_constraint(v, pltpu.HBM)
            for v in (
                hidden_in, norm_gain[None, :], norm_shift[None, :],
                jnp.transpose(attend_weight, (1, 0, 2)), output_weight, up_weight,
                up_bias[None, :], down_weight, down_bias[None, :], key_cache, value_cache, freq,
                cached_len,
            )
        ]
    )


def solution(mesh):
    placed = (
        P("req", "head"), P(), P(), P(None, None, "head"), P("head", None), P("req", "head"),
        P("head"), P("head", "req"), P("head"), P("req", None, "head"), P("req", None, "head"), P("req"),
    )
    return jax.shard_map(
        body,
        mesh=mesh,
        in_specs=placed,
        out_specs=(P("req", "head"), P("req", None, "head"), P("req", None, "head")),
        check_vma=False,
    )
```
